128 devices in a mesh: row: 8 (over y_hi, z), col: 16 (over x, y_lo, core).
Axes of the slice: x: 4, y: 4 (y_hi: 2, y_lo: 2; y = y_hi * 2 + y_lo), z: 4, core: 2. Of those that a mesh axis runs over, the one named last changes fastest.
Arguments:
- images: bfloat16 [128, 3, 128, 192], P(('row', 'col')), may hold values from -1000 to 1000
- weights: bfloat16 [32, 48, 128, 1200], P('row', 'col'), may hold values from -0.1875 to 0.1875
Outputs:
- weight_grad: float32 [32, 48, 128, 1200], P('row', 'col')
The draws below stay inside these ranges and needn't reach their ends.
All inputs are finite; a program needn't handle non-finite values.
Results may differ from the reference program's by a relative error of at most 0.006.
Values may be sent and summed in bfloat16 or wider, within the bound.
A program may use at most 128 MiB of HBM per device.

```python
import math
import jax
import jax.numpy as jnp
from jax import lax

B = 128
CH = 3
S = 4
FIELD = 20
F = 128
PAD = 8
K = 1200
PROWS = 32
PCOLS = 48
HEIGHT = 128
WIDTH = 192


def draw_images(key, part):
    streams = jax.random.split(key, 5)
    log_scale = jax.random.uniform(streams[0], (B, 1, 1, 1), jnp.float32, 0.0, math.log(10.0))
    shifts = jax.random.uniform(streams[1], (B, CH, 1, 1), jnp.float32, -3.0, 3.0)
    row_scale = jnp.exp(jax.random.uniform(streams[2], (B, 1, HEIGHT, 1), jnp.float32, 0.0, math.log(4.0)))
    col_scale = jnp.exp(jax.random.uniform(streams[3], (B, 1, 1, WIDTH), jnp.float32, 0.0, math.log(4.0)))
    jitter = jnp.clip(jax.random.normal(streams[4], (B, CH, HEIGHT, WIDTH), jnp.float32), -6.0, 6.0)
    return (shifts + jnp.exp(log_scale) * row_scale * col_scale * jitter).astype(jnp.bfloat16)


def steps_of(rng, shape, shards, least, largest):
    def one(position, blocks):
        steps = jax.random.uniform(jax.random.fold_in(jax.random.fold_in(rng, 6), position), (blocks,), jnp.float32, least / len(shards), largest / len(shards))
        return jnp.repeat(jnp.exp(steps), shape[position] // blocks).reshape((-1,) + (1,) * (len(shape) - position - 1))

    factor_of = one(*shards[0])
    for cut in shards[1:]:
        factor_of = factor_of * one(*cut)
    return factor_of


def scatter_about(stream_key, shape, scale, most, cuts=(), held_as=jnp.bfloat16):
    result = jax.random.normal(stream_key, shape, jnp.float32) * scale
    if len(cuts) > 0:
        result = steps_of(stream_key, shape, cuts, -0.22, 0.18) * result
    return jnp.clip(result, min=-most, max=most).astype(held_as)


def setup_inputs(seed: int = 0) -> dict:
    seeds = jax.random.split(jax.random.key(seed), 3)
    return {
        "images": draw_images(jax.random.fold_in(seeds[2], 71), 0),
        "weights": scatter_about(seeds[1], (PROWS, PCOLS, F, K), K ** -0.5, 0.1875, ((0, 8), (1, 16))),
    }


sparsity = 0.5

def field_rows(padded, prow):
    band = lax.dynamic_slice_in_dim(padded, prow * S, FIELD, axis=1)
    table = S * jnp.arange(PCOLS, dtype=jnp.int32)[:, None] + jnp.arange(FIELD, dtype=jnp.int32)[None, :]
    picked = band[:, :, table, :]
    picked = jnp.transpose(picked, (2, 0, 1, 3, 4))
    return picked.reshape(PCOLS, K, picked.shape[-1])

def box_sum(values):
    padded = jnp.pad(values, ((1, 1), (1, 1), (0, 0), (0, 0)))
    total = jnp.zeros(values.shape, jnp.float32)
    for down in range(3):
        for across in range(3):
            total = total + padded[down:down + PROWS, across:across + PCOLS]
    return total

def reference(images, weights):
    pixels = images.astype(jnp.float32)
    center = lax.optimization_barrier(jnp.mean(pixels, axis=(1, 2, 3), keepdims=True))
    variance = lax.optimization_barrier(jnp.mean(jnp.square(pixels - center), axis=(1, 2, 3), keepdims=True))
    normed = ((pixels - center) / jnp.sqrt(variance + 1e-05)).astype(jnp.bfloat16)
    plane = jnp.transpose(normed, (1, 2, 3, 0))
    padded = jnp.pad(plane, ((0, 0), (PAD, PAD), (PAD, PAD), (0, 0)))
    positions = jnp.arange(PROWS, dtype=jnp.int32)

    def encode(prow):
        patches = field_rows(padded, prow).astype(jnp.float32)
        return jnp.einsum('qfk,qkb->qfb', weights[prow].astype(jnp.float32), patches).astype(jnp.bfloat16)
    hidden = lax.map(encode, positions)
    squares = jnp.square(hidden.astype(jnp.float32))
    energy = jnp.sqrt(1.0 + box_sum(squares))
    inverse = (1.0 / energy).astype(jnp.bfloat16)
    spread = box_sum(inverse.astype(jnp.float32))
    table = S * jnp.arange(PCOLS, dtype=jnp.int32)[:, None] + jnp.arange(FIELD, dtype=jnp.int32)[None, :]

    def place(total, prow):
        terms = jnp.einsum('qfk,qfb->qkb', weights[prow].astype(jnp.float32), hidden[prow].astype(jnp.float32))
        terms = terms.reshape(PCOLS, CH, FIELD, FIELD, terms.shape[-1]).transpose(1, 2, 0, 3, 4)
        band = lax.dynamic_slice_in_dim(total, prow * S, FIELD, axis=1)
        band = band.at[:, :, table, :].add(terms)
        return (lax.dynamic_update_slice_in_dim(total, band, prow * S, axis=1), None)
    total, _ = lax.scan(place, jnp.zeros(padded.shape, jnp.float32), positions)
    recon = total[:, PAD:PAD + HEIGHT, PAD:PAD + WIDTH]
    residual = (recon - plane.astype(jnp.float32)).astype(jnp.bfloat16)
    resid_pad = jnp.pad(residual, ((0, 0), (PAD, PAD), (PAD, PAD), (0, 0)))

    def gradient(prow):
        image_patches = field_rows(padded, prow).astype(jnp.float32)
        resid_patches = field_rows(resid_pad, prow).astype(jnp.float32)
        weight_row = weights[prow].astype(jnp.float32)
        hidden_row = hidden[prow].astype(jnp.float32)
        back = sparsity * hidden_row * spread[prow] + jnp.einsum('qfk,qkb->qfb', weight_row, resid_patches)
        back = lax.optimization_barrier(back.astype(jnp.bfloat16)).astype(jnp.float32)
        grad = jnp.einsum('qfb,qkb->qfk', back, image_patches) + jnp.einsum('qfb,qkb->qfk', hidden_row, resid_patches)
        return grad / B
    return lax.map(gradient, positions)
```

```python
import jax
import jax.numpy as jnp
from jax import lax
from jax.experimental import pallas as pl
from jax.experimental.pallas import tpu as pltpu
from jax.sharding import PartitionSpec as P

MESH = pl.DeviceIdType.MESH
F32 = jnp.float32
BF16 = jnp.bfloat16

ROWS, COLS = 8, 16
DEVS = ROWS * COLS
CH, S, FIELD, PAD = 3, 4, 20, 8
K = 1200
F = 128
B = 128
HEIGHT, WIDTH = 128, 192
PR, PC = 4, 3
SPARSITY = 0.5
EPS = 1e-05

DIRS = [(dr, dc) for dr in (-1, 0, 1) for dc in (-1, 0, 1) if (dr, dc) != (0, 0)]
OPP = [DIRS.index((-dr, -dc)) for dr, dc in DIRS]
ORDER = sorted(range(8), key=lambda k: DIRS[k][1] != 0)


def rim_rows(k):
    dr, dc = DIRS[k]
    ny = 16 if dr == 0 else 8
    nx = 16 if dc == 0 else 8
    return ny, nx


def rim(d, starts, wide):
    return (8, 16) if d == 0 else (starts[d], wide)


def outer(k):
    dr, dc = DIRS[k]
    y0 = {-1: 0, 0: 8, 1: 24}[dr]
    x0 = {-1: 0, 0: 8, 1: 20}[dc]
    ny, nx = rim_rows(k)
    return slice(y0, y0 + ny), slice(x0, x0 + nx)


def inner(k):
    dr, dc = DIRS[k]
    y0 = {-1: 8, 0: 8, 1: 16}[dr]
    x0 = {-1: 8, 0: 8, 1: 12}[dc]
    ny, nx = rim_rows(k)
    return slice(y0, y0 + ny), slice(x0, x0 + nx)


def pos_src(d, n):
    return {-1: slice(1, 2), 0: slice(1, n + 1), 1: slice(n, n + 1)}[d]


def pos_dst(d, n):
    return {-1: slice(n + 1, n + 2), 0: slice(1, n + 1), 1: slice(0, 1)}[d]


def main_kernel(img, w_hbm, pat, lhs, *scr):
    (wt, wv, nf, sb, rb, ext, rext, cext, tmp, hext, iext, hs) = scr[:12]
    snd_a, rcv_a, snd_b, rcv_b = scr[12:20], scr[20:28], scr[28:36], scr[36:44]
    (w_sem, a2a_send, a2a_recv, h_send, h_recv, i_send, i_recv, ca_send, ca_recv, cb_send, cb_recv) = scr[44:]
    row = lax.axis_index("row")
    col = lax.axis_index("col")
    me = row * COLS + col

    for ref in (hext, iext):
        ref[...] = jnp.zeros(ref.shape, ref.dtype)
    for ref in (*rcv_a, *rcv_b):
        ref[...] = jnp.zeros(ref.shape, ref.dtype)

    barrier = pltpu.get_barrier_semaphore()

    def greet(i, carry):
        t = lax.rem(me + i, DEVS)
        pl.semaphore_signal(
            barrier, inc=1, device_id=(lax.div(t, COLS), lax.rem(t, COLS)), device_id_type=MESH
        )
        return carry

    lax.fori_loop(1, DEVS, greet, 0)

    w_copy = pltpu.make_async_copy(w_hbm, wt, w_sem)
    w_copy.start()

    pixels = img[...].reshape(CH * WIDTH, HEIGHT).astype(F32)
    count = CH * HEIGHT * WIDTH
    center = jnp.sum(pixels, axis=(0, 1), keepdims=True) / count
    shifted = pixels - center
    variance = jnp.sum(shifted * shifted, axis=(0, 1), keepdims=True) / count
    normed = shifted / jnp.sqrt(variance + EPS)
    for c in range(CH):
        plane = normed[c * WIDTH : (c + 1) * WIDTH]
        rows = slice(c * HEIGHT, (c + 1) * HEIGHT)
        nf[0, rows, :] = plane[0:128].T
        nf[1, rows, 0:64] = plane[128:192].T
        nf[1, rows, 64:128] = jnp.zeros((HEIGHT, 64), F32)

    fold = jnp.concatenate(
        [nf[half, pl.ds(j, 96, stride=4), :] for j in range(4) for half in range(2)], axis=1
    ).astype(BF16)
    apart = lax.broadcasted_iota(jnp.int32, (128, 128), 0) - lax.broadcasted_iota(
        jnp.int32, (128, 128), 1
    )
    lane = lax.broadcasted_iota(jnp.int32, (128, 128), 1)

    def cut(t, carry):
        picks = []
        for j in range(4):
            here = (lane >= 32 * j) & (lane < 32 * j + 28)
            for half in range(2):
                hit = here & (apart == 12 * t - 8 - 32 * j - 128 * half)
                picks.append(jnp.where(hit, 1.0, 0.0).astype(BF16))
        pick = jnp.concatenate(picks, axis=0)
        block = jnp.dot(fold, pick, preferred_element_type=F32).astype(BF16)
        view = sb.at[t].reshape(CH * 64, 128)
        for c in range(CH):
            view[c * 64 : c * 64 + 16, :] = jnp.zeros((16, 128), BF16)
            view[c * 64 + 16 : c * 64 + 48, :] = block[c * 32 : c * 32 + 32]
            view[c * 64 + 48 : c * 64 + 64, :] = jnp.zeros((16, 128), BF16)
        return carry

    lax.fori_loop(0, COLS, cut, 0)

    pl.semaphore_wait(barrier, DEVS - 1)

    own = pltpu.make_async_copy(
        sb.at[col, :, pl.ds(7 + 2 * row, 4)], rb.at[:, :, me], a2a_recv
    )
    own.start()

    def send_block(i, carry):
        t = lax.rem(me + i, DEVS)
        tr = lax.div(t, COLS)
        tc = lax.rem(t, COLS)
        pltpu.make_async_remote_copy(
            src_ref=sb.at[tc, :, pl.ds(7 + 2 * tr, 4)],
            dst_ref=rb.at[:, :, me],
            send_sem=a2a_send,
            recv_sem=a2a_recv,
            device_id=(tr, tc),
            device_id_type=MESH,
        ).start()
        return carry

    lax.fori_loop(1, DEVS, send_block, 0)

    rext[...] = jnp.zeros(rext.shape, F32)
    cext[...] = jnp.zeros(cext.shape, F32)
    w_copy.wait()

    def flip(pos, carry):
        for kb in range(0, K, 128):
            n = min(128, K - kb)
            wv[pos, :, kb : kb + n] = wt[pos, kb : kb + n, :].T
        return carry

    lax.fori_loop(0, PR * PC, flip, 0)

    mr = lax.broadcasted_iota(jnp.int32, (256, 256), 0)
    mc = lax.broadcasted_iota(jnp.int32, (256, 256), 1)
    split = jnp.where(
        mr == jnp.where(mc < 128, 2 * mc, 2 * mc - 255), 1.0, 0.0
    ).astype(BF16)

    pltpu.make_async_copy(rb, rb, a2a_recv).wait()

    for c in range(CH):
        for i in range(4):
            pair = rb.at[c, i].reshape(256, 128)[...]
            turned = lax.dot_general(
                pair, split, (((0,), (0,)), ((), ())), preferred_element_type=F32
            )
            for par in range(2):
                y0 = 8 * i + 4 * par
                ext[c, y0 : y0 + 4] = turned[:, par * 128 : par * 128 + 128].reshape(4, 32, 128)

    def patch(src, base, p, q):
        for j in range(CH * FIELD):
            c, u = divmod(j, FIELD)
            tmp[pl.ds(base + FIELD * j, FIELD), :] = src[c, S * p + u, pl.ds(S * q, FIELD), :]
        return tmp[pl.ds(pl.multiple_of(base, 8), K), :].astype(BF16)

    def forward(pos, carry):
        p = lax.div(pos, PC)
        q = pos - PC * p
        base = lax.rem(pos, 2) * K
        columns = patch(ext, base, p, q)
        pat[pos, :, 0:128] = columns
        hidden = jnp.dot(wv[pos], columns, preferred_element_type=F32).astype(BF16)
        hext[p + 1, q + 1] = hidden
        terms = jnp.dot(wt[pos], hidden, preferred_element_type=F32)
        tmp[pl.ds(pl.multiple_of(base, 8), K), :] = terms
        for j in range(CH * FIELD):
            c, u = divmod(j, FIELD)
            cext[c, S * p + u, pl.ds(S * q, FIELD), :] += tmp[pl.ds(base + FIELD * j, FIELD), :]
        return carry

    lax.fori_loop(0, PR * PC, forward, 0)

    def there(k):
        dr, dc = DIRS[k]
        ok = None
        for d, at, n in ((dr, row, ROWS), (dc, col, COLS)):
            if d:
                one = at > 0 if d < 0 else at < n - 1
                ok = one if ok is None else ok & one
        return ok

    def link(k, src, dst, send, recv):
        dr, dc = DIRS[k]
        return pltpu.make_async_remote_copy(
            src_ref=src,
            dst_ref=dst,
            send_sem=send.at[k],
            recv_sem=recv.at[k],
            device_id=(row + dr, col + dc),
            device_id_type=MESH,
        )

    def halo(k, ref, send, recv):
        dr, dc = DIRS[k]
        return link(
            k,
            ref.at[pos_src(dr, PR), pos_src(dc, PC)],
            ref.at[pos_dst(dr, PR), pos_dst(dc, PC)],
            send,
            recv,
        )

    def start_all(make):
        for k in range(8):
            @pl.when(there(k))
            def _(k=k):
                make(k).start()

    def arrive_all(make):
        for k in range(8):
            @pl.when(there(k))
            def _(k=k):
                make(OPP[k]).wait_recv()

    def sent_all(make):
        for k in range(8):
            @pl.when(there(k))
            def _(k=k):
                make(k).wait_send()

    def hidden_link(k):
        return halo(k, hext, h_send, h_recv)

    def inverse_link(k):
        return halo(k, iext, i_send, i_recv)

    def contrib_link(k):
        return link(k, snd_a[k], rcv_a[k], ca_send, ca_recv)

    def resid_link(k):
        return link(k, snd_b[k], rcv_b[k], cb_send, cb_recv)

    for k in range(8):
        ys, xs = outer(k)
        snd_a[k][...] = cext[:, ys, xs, :].reshape(snd_a[k].shape).astype(BF16)
    start_all(contrib_link)
    start_all(hidden_link)

    arrive_all(hidden_link)

    def box(get, rows_out, cols_out):
        grid = [[get(a, b) for b in range(cols_out + 2)] for a in range(rows_out + 2)]
        tall = [
            [grid[a][b] + grid[a + 1][b] + grid[a + 2][b] for b in range(cols_out + 2)]
            for a in range(rows_out)
        ]
        return [
            [tall[a][b] + tall[a][b + 1] + tall[a][b + 2] for b in range(cols_out)]
            for a in range(rows_out)
        ]

    def pool(n, carry):
        rows16 = pl.ds(pl.multiple_of(n * 16, 16), 16)

        def square(a, b):
            v = hext[a, b, rows16, :].astype(F32)
            return v * v

        sums = box(square, PR, PC)
        for a in range(PR):
            for b in range(PC):
                energy = jnp.sqrt(1.0 + sums[a][b])
                iext[a + 1, b + 1, rows16, :] = (1.0 / energy).astype(BF16)
        return carry

    lax.fori_loop(0, 8, pool, 0)
    start_all(inverse_link)

    arrive_all(contrib_link)
    for k in range(8):
        ys, xs = inner(k)
        ny, nx = rim_rows(k)
        cext[:, ys, xs, :] += rcv_a[OPP[k]][...].astype(F32).reshape(CH, ny, nx, 128)
    for xs in (slice(8, 16), slice(16, 20)):
        resid = cext[:, 8:24, xs, :] - ext[:, 8:24, xs, :]
        rext[:, 8:24, xs, :] = resid.astype(BF16).astype(F32)
    for k in range(8):
        ys, xs = inner(k)
        snd_b[k][...] = rext[:, ys, xs, :].reshape(snd_b[k].shape).astype(BF16)
    start_all(resid_link)

    arrive_all(inverse_link)

    def widen(n, carry):
        rows16 = pl.ds(pl.multiple_of(n * 16, 16), 16)
        sums = box(lambda a, b: iext[a, b, rows16, :].astype(F32), PR, PC)
        for a in range(PR):
            for b in range(PC):
                hidden = hext[a + 1, b + 1, rows16, :]
                lhs[a * PC + b, rows16, 128:256] = hidden
                hs[a * PC + b, rows16, :] = SPARSITY * hidden.astype(F32) * sums[a][b]
        return carry

    lax.fori_loop(0, 8, widen, 0)

    arrive_all(resid_link)
    for k in ORDER:
        ys, xs = outer(k)
        ny, nx = rim_rows(k)
        got = rcv_b[OPP[k]][...].astype(F32).reshape(CH, ny, nx, 128)
        if nx == 16:
            rext[:, ys, 8:16, :] = got[:, :, 0:8]
            rext[:, ys, 16:20, :] = got[:, :, 8:12]
        else:
            rext[:, ys, xs, :] = got

    def backward(pos, carry):
        p = lax.div(pos, PC)
        q = pos - PC * p
        base = lax.rem(pos, 2) * K
        columns = patch(rext, base, p, q)
        pat[pos, :, 128:256] = columns
        back = hs[pos] + jnp.dot(wv[pos], columns, preferred_element_type=F32)
        lhs[pos, :, 0:128] = back.astype(BF16)
        return carry

    lax.fori_loop(0, PR * PC, backward, 0)

    pltpu.make_async_copy(
        rb.at[:, :, pl.ds(0, DEVS - 1)], rb.at[:, :, pl.ds(0, DEVS - 1)], a2a_send
    ).wait()
    for make in (hidden_link, inverse_link, contrib_link, resid_link):
        sent_all(make)


def grad_kernel(pat, lhs, out):
    pos = pl.program_id(0)
    grad = lax.dot_general(
        pat[pos], lhs[pos], (((1,), (1,)), ((), ())), preferred_element_type=F32
    )
    out[0] = grad * (1.0 / B)


def main_call(images, weights):
    rims = [CH * rim_rows(k)[0] * rim_rows(k)[1] for k in range(8)]
    bufs = [pltpu.VMEM((n, 128), BF16) for n in rims]
    dma = pltpu.SemaphoreType.DMA
    vmem = pl.BlockSpec(memory_space=pltpu.VMEM)
    n_pos = PR * PC
    return pl.pallas_call(
        main_kernel,
        name="rica_main",
        out_shape=(pltpu.VMEM((n_pos, K, 256), BF16), pltpu.VMEM((n_pos, F, 256), BF16)),
        in_specs=[vmem, pl.BlockSpec(memory_space=pltpu.HBM)],
        out_specs=(vmem, vmem),
        scratch_shapes=[
            pltpu.VMEM((n_pos, K, F), BF16),
            pltpu.VMEM((n_pos, F, K), BF16),
            pltpu.VMEM((2, CH * HEIGHT, 128), F32),
            pltpu.VMEM((COLS, CH, 32, 2, 128), BF16),
            pltpu.VMEM((CH, 4, DEVS, 2, 128), BF16),
            pltpu.VMEM((CH, 32, 32, 128), F32),
            pltpu.VMEM((CH, 32, 32, 128), F32),
            pltpu.VMEM((CH, 32, 32, 128), F32),
            pltpu.VMEM((2 * K, 128), F32),
            pltpu.VMEM((PR + 2, PC + 2, F, B), BF16),
            pltpu.VMEM((PR + 2, PC + 2, F, B), BF16),
            pltpu.VMEM((n_pos, F, B), F32),
            *bufs,
            *bufs,
            *bufs,
            *bufs,
            dma,
            dma,
            dma,
            *[dma((8,)) for _ in range(8)],
        ],
        compiler_params=pltpu.CompilerParams(
            collective_id=0, has_side_effects=True, vmem_limit_bytes=40 * 1024 * 1024
        ),
    )(images, weights)


def grad_call(pat, lhs):
    n_pos = PR * PC
    vmem = pl.BlockSpec(memory_space=pltpu.VMEM)
    return pl.pallas_call(
        grad_kernel,
        name="rica_grad",
        grid=(n_pos,),
        out_shape=jax.ShapeDtypeStruct((n_pos, K, F), F32),
        in_specs=[vmem, vmem],
        out_specs=pl.BlockSpec((1, K, F), lambda i: (i, 0, 0)),
        compiler_params=pltpu.CompilerParams(vmem_limit_bytes=12 * 1024 * 1024),
    )(pat, lhs)


def body(images, weights):
    images = images.reshape(CH, HEIGHT, WIDTH).transpose(0, 2, 1)
    weights = weights.reshape(PR * PC, F, K).transpose(0, 2, 1)
    weights = pltpu.with_memory_space_constraint(weights, pltpu.HBM)
    pat, lhs = main_call(images, weights)
    pat = pltpu.with_memory_space_constraint(pat, pltpu.VMEM)
    lhs = pltpu.with_memory_space_constraint(lhs, pltpu.VMEM)
    grad = grad_call(pat, lhs)
    return grad.transpose(0, 2, 1).reshape(PR, PC, F, K)


def solution(mesh):
    return jax.shard_map(
        body,
        mesh=mesh,
        in_specs=(P(("row", "col"), None, None, None), P("row", "col", None, None)),
        out_specs=P("row", "col", None, None),
        check_vma=False,
    )
```

```python
import jax
import jax.numpy as jnp
from jax import lax
from jax.experimental import pallas as pl
from jax.experimental.pallas import tpu as pltpu
from jax.sharding import PartitionSpec as P

MESH = pl.DeviceIdType.MESH
F32 = jnp.float32
BF16 = jnp.bfloat16

ROWS, COLS = 8, 16
DEVS = ROWS * COLS
CH, S, FIELD, PAD = 3, 4, 20, 8
K = 1200
F = 128
B = 128
HEIGHT, WIDTH = 128, 192
PR, PC = 4, 3
SPARSITY = 0.5
EPS = 1e-05

DIRS = [(dr, dc) for dr in (-1, 0, 1) for dc in (-1, 0, 1) if (dr, dc) != (0, 0)]
OPP = [DIRS.index((-dr, -dc)) for dr, dc in DIRS]
ORDER = sorted(range(8), key=lambda k: DIRS[k][1] != 0)


def rim_rows(k):
    dr, dc = DIRS[k]
    ny = 16 if dr == 0 else 8
    nx = 16 if dc == 0 else 8
    return ny, nx


def rim(d, starts, wide):
    return (8, 16) if d == 0 else (starts[d], wide)


def outer(k):
    dr, dc = DIRS[k]
    y0 = {-1: 0, 0: 8, 1: 24}[dr]
    x0 = {-1: 8, 0: 16, 1: 28}[dc]
    ny, nx = rim_rows(k)
    return slice(y0, y0 + ny), slice(x0, x0 + nx)


def inner(k):
    dr, dc = DIRS[k]
    y0 = {-1: 8, 0: 8, 1: 16}[dr]
    x0 = {-1: 16, 0: 16, 1: 20}[dc]
    ny, nx = rim_rows(k)
    return slice(y0, y0 + ny), slice(x0, x0 + nx)


def pos_src(d, n):
    return {-1: slice(1, 2), 0: slice(1, n + 1), 1: slice(n, n + 1)}[d]


def pos_dst(d, n):
    return {-1: slice(n + 1, n + 2), 0: slice(1, n + 1), 1: slice(0, 1)}[d]


def main_kernel(img_hbm, w_hbm, pat, rpat, back_out, hid_out, *scr):
    (img, wt, wv, strip, sb, rb, ext, rext, cext, hext, iext, hs) = scr[:12]
    snd_a, rcv_a, snd_b, rcv_b = scr[12:20], scr[20:28], scr[28:36], scr[36:44]
    (im_sem, w_sem, a2a_send, a2a_recv, h_send, h_recv, i_send, i_recv, ca_send, ca_recv, cb_send, cb_recv) = scr[44:]
    row = lax.axis_index("row")
    col = lax.axis_index("col")
    me = row * COLS + col

    im_copy = pltpu.make_async_copy(img_hbm, img, im_sem)
    im_copy.start()

    def there(k):
        dr, dc = DIRS[k]
        ok = None
        for d, at, n in ((dr, row, ROWS), (dc, col, COLS)):
            if d:
                one = at > 0 if d < 0 else at < n - 1
                ok = one if ok is None else ok & one
        return ok

    for k in range(8):

        @pl.when(jnp.logical_not(there(k)))
        def _(k=k):
            dr, dc = DIRS[OPP[k]]
            for ref in (hext, iext):
                for a in range(*pos_dst(dr, PR).indices(PR + 2)):
                    for b in range(*pos_dst(dc, PC).indices(PC + 2)):
                        ref[a, b] = jnp.zeros((F, B), BF16)
            for ref in (rcv_a[OPP[k]], rcv_b[OPP[k]]):
                ref[...] = jnp.zeros(ref.shape, BF16)

    barrier = pltpu.get_barrier_semaphore()

    def greet(i, carry):
        tr = (row + i) & (ROWS - 1)
        for j in range(COLS):
            pl.semaphore_signal(
                barrier, inc=1, device_id=(tr, (col + j) & (COLS - 1)), device_id_type=MESH
            )
        return carry

    lax.fori_loop(1, ROWS, greet, 0)
    for j in range(1, COLS):
        pl.semaphore_signal(
            barrier, inc=1, device_id=(row, (col + j) & (COLS - 1)), device_id_type=MESH
        )

    w_copy = pltpu.make_async_copy(w_hbm, wt, w_sem)
    w_copy.start()

    im_copy.wait()
    pixels = img[...].reshape(CH * WIDTH, HEIGHT).astype(F32)
    count = CH * HEIGHT * WIDTH
    center = jnp.sum(pixels, axis=(0, 1), keepdims=True) / count
    shifted = pixels - center
    variance = jnp.sum(shifted * shifted, axis=(0, 1), keepdims=True) / count
    normed = (shifted / jnp.sqrt(variance + EPS)).astype(BF16)

    planes = jnp.concatenate([normed[c * WIDTH : (c + 1) * WIDTH] for c in range(CH)], axis=1)
    yy = lax.broadcasted_iota(jnp.int32, (HEIGHT, 128), 0)
    lane = lax.broadcasted_iota(jnp.int32, (HEIGHT, 128), 1)
    where_from = []
    for c in range(CH):
        offset = jnp.where((lane >> 5) == c, yy - 4 * (lane & 31), -1)
        where_from.append(
            jnp.concatenate([jnp.where(offset == j, 1.0, 0.0) for j in range(4)], axis=1)
        )
    spread_y = jnp.concatenate(where_from, axis=0).astype(BF16)
    strips = jnp.dot(planes, spread_y, preferred_element_type=F32)
    for j in range(4):
        strip[j, 0:8, :] = jnp.zeros((8, 128), F32)
        strip[j, 8 : 8 + WIDTH, :] = strips[:, j * 128 : j * 128 + 128]
        strip[j, 8 + WIDTH : 32 + WIDTH, :] = jnp.zeros((24, 128), F32)

    def cut(t, carry):
        parts = [strip[j, pl.ds(12 * t, 32), :] for j in range(4)]
        block = jnp.concatenate(parts, axis=0).astype(BF16).T
        view = sb.at[t].reshape(CH * 64, 128)
        for c in range(CH):
            view[c * 64 : c * 64 + 16, :] = jnp.zeros((16, 128), BF16)
            view[c * 64 + 16 : c * 64 + 48, :] = block[c * 32 : c * 32 + 32]
            view[c * 64 + 48 : c * 64 + 64, :] = jnp.zeros((16, 128), BF16)
        return carry

    lax.fori_loop(0, COLS, cut, 0)

    pl.semaphore_wait(barrier, DEVS - 1)

    own = pltpu.make_async_copy(
        sb.at[col, :, pl.ds(7 + 2 * row, 4)], rb.at[:, :, me], a2a_recv
    )
    own.start()

    def send_block(tr, tc):
        pltpu.make_async_remote_copy(
            src_ref=sb.at[tc, :, pl.ds(7 + 2 * tr, 4)],
            dst_ref=rb.at[:, :, me],
            send_sem=a2a_send,
            recv_sem=a2a_recv,
            device_id=(tr, tc),
            device_id_type=MESH,
        ).start()

    def send_row(i, carry):
        tr = (row + i) & (ROWS - 1)
        for j in range(COLS):
            send_block(tr, (col + j) & (COLS - 1))
        return carry

    lax.fori_loop(1, ROWS, send_row, 0)
    for j in range(1, COLS):
        send_block(row, (col + j) & (COLS - 1))

    cext[...] = jnp.zeros(cext.shape, F32)
    w_copy.wait()

    def flip(pos, carry):
        for kb in range(0, K, 128):
            n = min(128, K - kb)
            wv[pos, :, kb : kb + n] = wt[pos, kb : kb + n, :].T
        return carry

    lax.fori_loop(0, PR * PC, flip, 0)

    mr = lax.broadcasted_iota(jnp.int32, (256, 256), 0)
    mc = lax.broadcasted_iota(jnp.int32, (256, 256), 1)
    split = jnp.where(
        mr == jnp.where(mc < 128, 2 * mc, 2 * mc - 255), 1.0, 0.0
    ).astype(BF16)

    pltpu.make_async_copy(rb, rb, a2a_recv).wait()

    for c in range(CH):
        for i in range(4):
            pair = rb.at[c, i].reshape(256, 128)[...]
            turned = lax.dot_general(
                pair, split, (((0,), (0,)), ((), ())), preferred_element_type=F32
            )
            for par in range(2):
                y0 = 8 * i + 4 * par
                ext[c, y0 : y0 + 4, 8:40, :] = turned[:, par * 128 : par * 128 + 128].reshape(4, 32, 128)

    low = lax.broadcasted_iota(jnp.int32, (8, 128), 0) < 4

    def patch(src, p, x0):
        blocks = []
        for c in range(CH):
            for u in range(0, FIELD, 2):
                y = S * p + u
                blocks += [
                    src[c, y, pl.ds(x0, 8), :],
                    src[c, y, pl.ds(x0 + 8, 8), :],
                    jnp.where(low, src[c, y, pl.ds(x0 + 16, 8), :], src[c, y + 1, pl.ds(x0 - 4, 8), :]),
                    src[c, y + 1, pl.ds(x0 + 4, 8), :],
                    src[c, y + 1, pl.ds(x0 + 12, 8), :],
                ]
        return jnp.concatenate(blocks, axis=0).astype(BF16)

    def unpatch(dst, terms, p, x0):
        blocks = [terms[8 * m : 8 * m + 8] for m in range(K // 8)]
        for c in range(CH):
            for u in range(0, FIELD, 2):
                y = S * p + u
                b0, b1, b2, b3, b4 = blocks[(c * FIELD + u) // 2 * 5 :][:5]
                dst[c, y, pl.ds(x0, 8), :] += b0
                dst[c, y, pl.ds(x0 + 8, 8), :] += b1
                dst[c, y, pl.ds(x0 + 16, 8), :] += jnp.where(low, b2, 0.0)
                dst[c, y + 1, pl.ds(x0 - 4, 8), :] += jnp.where(low, 0.0, b2)
                dst[c, y + 1, pl.ds(x0 + 4, 8), :] += b3
                dst[c, y + 1, pl.ds(x0 + 12, 8), :] += b4

    def encode(p, carry):
        zero = lax.shift_right_logical(p, 4)
        for q in range(PC):
            pos = PC * p + q
            columns = patch(ext, p, zero + (8 + S * q))
            pat[pos] = columns
            hidden = jnp.dot(wv[pos], columns, preferred_element_type=F32).astype(BF16)
            hext[p + 1, q + 1] = hidden
            hid_out[pos] = hidden
        return carry

    lax.fori_loop(0, PR, encode, 0)

    def link(k, src, dst, send, recv):
        dr, dc = DIRS[k]
        return pltpu.make_async_remote_copy(
            src_ref=src,
            dst_ref=dst,
            send_sem=send.at[k],
            recv_sem=recv.at[k],
            device_id=(row + dr, col + dc),
            device_id_type=MESH,
        )

    def halo(k, ref, send, recv):
        dr, dc = DIRS[k]
        return link(
            k,
            ref.at[pos_src(dr, PR), pos_src(dc, PC)],
            ref.at[pos_dst(dr, PR), pos_dst(dc, PC)],
            send,
            recv,
        )

    def start_all(make):
        for k in range(8):
            @pl.when(there(k))
            def _(k=k):
                make(k).start()

    def arrive_all(make):
        for k in range(8):
            @pl.when(there(k))
            def _(k=k):
                make(OPP[k]).wait_recv()

    def sent_all(make):
        for k in range(8):
            @pl.when(there(k))
            def _(k=k):
                make(k).wait_send()

    def hidden_link(k):
        return halo(k, hext, h_send, h_recv)

    def inverse_link(k):
        return halo(k, iext, i_send, i_recv)

    def contrib_link(k):
        return link(k, snd_a[k], rcv_a[k], ca_send, ca_recv)

    def resid_link(k):
        return link(k, snd_b[k], rcv_b[k], cb_send, cb_recv)

    start_all(hidden_link)

    def decode(p, carry):
        zero = lax.shift_right_logical(p, 4)
        for q in range(PC):
            pos = PC * p + q
            terms = jnp.dot(wt[pos], hid_out[pos], preferred_element_type=F32)
            unpatch(cext, terms, p, zero + (8 + S * q))
        return carry

    lax.fori_loop(0, PR, decode, 0)

    for k in range(8):
        ys, xs = outer(k)
        snd_a[k][...] = cext[:, ys, xs, :].reshape(snd_a[k].shape).astype(BF16)
    start_all(contrib_link)

    arrive_all(hidden_link)

    def box(get, rows_out, cols_out):
        grid = [[get(a, b) for b in range(cols_out + 2)] for a in range(rows_out + 2)]
        tall = [
            [grid[a][b] + grid[a + 1][b] + grid[a + 2][b] for b in range(cols_out + 2)]
            for a in range(rows_out)
        ]
        return [
            [tall[a][b] + tall[a][b + 1] + tall[a][b + 2] for b in range(cols_out)]
            for a in range(rows_out)
        ]

    def pool(n, carry):
        rows16 = pl.ds(pl.multiple_of(n * 16, 16), 16)

        def square(a, b):
            v = hext[a, b, rows16, :].astype(F32)
            return v * v

        sums = box(square, PR, PC)
        for a in range(PR):
            for b in range(PC):
                energy = jnp.sqrt(1.0 + sums[a][b])
                iext[a + 1, b + 1, rows16, :] = (1.0 / energy).astype(BF16)
        return carry

    lax.fori_loop(0, 8, pool, 0)
    start_all(inverse_link)

    arrive_all(contrib_link)
    for k in range(8):
        ys, xs = inner(k)
        ny, nx = rim_rows(k)
        cext[:, ys, xs, :] += rcv_a[OPP[k]][...].astype(F32).reshape(CH, ny, nx, 128)
    for xs in (slice(16, 24), slice(24, 28)):
        resid = cext[:, 8:24, xs, :] - ext[:, 8:24, xs, :]
        rext[:, 8:24, xs, :] = resid.astype(BF16).astype(F32)
    for k in range(8):
        ys, xs = inner(k)
        snd_b[k][...] = rext[:, ys, xs, :].reshape(snd_b[k].shape).astype(BF16)
    start_all(resid_link)

    arrive_all(inverse_link)

    def widen(n, carry):
        rows16 = pl.ds(pl.multiple_of(n * 16, 16), 16)
        sums = box(lambda a, b: iext[a, b, rows16, :].astype(F32), PR, PC)
        for a in range(PR):
            for b in range(PC):
                hidden = hid_out[a * PC + b, rows16, :]
                hs[a * PC + b, rows16, :] = SPARSITY * hidden.astype(F32) * sums[a][b]
        return carry

    lax.fori_loop(0, 8, widen, 0)

    arrive_all(resid_link)
    for k in ORDER:
        ys, xs = outer(k)
        ny, nx = rim_rows(k)
        got = rcv_b[OPP[k]][...].astype(F32).reshape(CH, ny, nx, 128)
        if nx == 16:
            rext[:, ys, 16:24, :] = got[:, :, 0:8]
            rext[:, ys, 24:28, :] = got[:, :, 8:12]
        else:
            rext[:, ys, xs, :] = got

    def backward(p, carry):
        zero = lax.shift_right_logical(p, 4)
        for q in range(PC):
            pos = PC * p + q
            columns = patch(rext, p, zero + (8 + S * q))
            rpat[pos] = columns
            back = hs[pos] + jnp.dot(wv[pos], columns, preferred_element_type=F32)
            back_out[pos] = back.astype(BF16)
        return carry

    lax.fori_loop(0, PR, backward, 0)

    pltpu.make_async_copy(
        rb.at[:, :, pl.ds(0, DEVS - 1)], rb.at[:, :, pl.ds(0, DEVS - 1)], a2a_send
    ).wait()
    for make in (hidden_link, inverse_link, contrib_link, resid_link):
        sent_all(make)


def grad_kernel(pat, rpat, back, hid, out, stage, sems):
    halves = (slice(0, K // 2), slice(K // 2, K))
    copies = []
    for pos in range(PR * PC):
        right = jnp.concatenate([back[pos], hid[pos]], axis=1)
        for n, rows in enumerate(halves):
            left = jnp.concatenate([pat[pos, rows, :], rpat[pos, rows, :]], axis=1)
            grad = lax.dot_general(left, right, (((1,), (1,)), ((), ())), preferred_element_type=F32)
            stage[pos, rows, :] = grad * (1.0 / B)
            copy = pltpu.make_async_copy(stage.at[pos, rows], out.at[pos, rows], sems.at[pos, n])
            copy.start()
            copies.append(copy)
    for copy in copies:
        copy.wait()


def main_call(images, weights):
    rims = [CH * rim_rows(k)[0] * rim_rows(k)[1] for k in range(8)]
    bufs = [pltpu.VMEM((n, 128), BF16) for n in rims]
    dma = pltpu.SemaphoreType.DMA
    vmem = pl.BlockSpec(memory_space=pltpu.VMEM)
    hbm = pl.BlockSpec(memory_space=pltpu.HBM)
    n_pos = PR * PC
    return pl.pallas_call(
        main_kernel,
        name="rica_main",
        out_shape=(
            pltpu.VMEM((n_pos, K, B), BF16),
            pltpu.VMEM((n_pos, K, B), BF16),
            pltpu.VMEM((n_pos, F, B), BF16),
            pltpu.VMEM((n_pos, F, B), BF16),
        ),
        in_specs=[hbm, hbm],
        out_specs=(vmem, vmem, vmem, vmem),
        scratch_shapes=[
            pltpu.VMEM((CH, WIDTH, HEIGHT), BF16),
            pltpu.VMEM((n_pos, K, F), BF16),
            pltpu.VMEM((n_pos, F, K), BF16),
            pltpu.VMEM((4, WIDTH + 32, 128), F32),
            pltpu.VMEM((COLS, CH, 32, 2, 128), BF16),
            pltpu.VMEM((CH, 4, DEVS, 2, 128), BF16),
            pltpu.VMEM((CH, 32, 40, 128), F32),
            pltpu.VMEM((CH, 32, 40, 128), F32),
            pltpu.VMEM((CH, 32, 40, 128), F32),
            pltpu.VMEM((PR + 2, PC + 2, F, B), BF16),
            pltpu.VMEM((PR + 2, PC + 2, F, B), BF16),
            pltpu.VMEM((n_pos, F, B), F32),
            *bufs,
            *bufs,
            *bufs,
            *bufs,
            *[dma for _ in range(4)],
            *[dma((8,)) for _ in range(8)],
        ],
        compiler_params=pltpu.CompilerParams(
            collective_id=0, has_side_effects=True, vmem_limit_bytes=36 * 1024 * 1024
        ),
    )(images, weights)


def grad_call(*factors):
    n_pos = PR * PC
    vmem = pl.BlockSpec(memory_space=pltpu.VMEM)
    return pl.pallas_call(
        grad_kernel,
        name="rica_grad",
        out_shape=jax.ShapeDtypeStruct((n_pos, K, F), F32),
        in_specs=[vmem] * 4,
        out_specs=pl.BlockSpec(memory_space=pltpu.HBM),
        scratch_shapes=[
            pltpu.VMEM((n_pos, K, F), F32),
            pltpu.SemaphoreType.DMA((n_pos, 2)),
        ],
        compiler_params=pltpu.CompilerParams(vmem_limit_bytes=12 * 1024 * 1024),
    )(*factors)


def body(images, weights):
    images = images.reshape(CH, HEIGHT, WIDTH).transpose(0, 2, 1)
    weights = weights.reshape(PR * PC, F, K).transpose(0, 2, 1)
    images = pltpu.with_memory_space_constraint(images, pltpu.HBM)
    weights = pltpu.with_memory_space_constraint(weights, pltpu.HBM)
    factors = main_call(images, weights)
    factors = [pltpu.with_memory_space_constraint(x, pltpu.VMEM) for x in factors]
    grad = grad_call(*factors)
    return grad.transpose(0, 2, 1).reshape(PR, PC, F, K)


def solution(mesh):
    return jax.shard_map(
        body,
        mesh=mesh,
        in_specs=(P(("row", "col"), None, None, None), P("row", "col", None, None)),
        out_specs=P("row", "col", None, None),
        check_vma=False,
    )
```

```python
import jax
import jax.numpy as jnp
from jax import lax
from jax.experimental import pallas as pl
from jax.experimental.pallas import tpu as pltpu
from jax.sharding import PartitionSpec as P

MESH = pl.DeviceIdType.MESH
F32 = jnp.float32
BF16 = jnp.bfloat16

ROWS, COLS = 8, 16
DEVS = ROWS * COLS
CH, S, FIELD, PAD = 3, 4, 20, 8
K = 1200
F = 128
B = 128
HEIGHT, WIDTH = 128, 192
PR, PC = 4, 3
SPARSITY = 0.5
EPS = 1e-05

SIDES = (0, 1)
OUTER = (8, 28)
INNER = (16, 20)
TOP = (0, 24)
EDGE = (8, 16)


def main_kernel(img_hbm, w_hbm, pat, rpat, back_out, hid_out, *scr):
    (img, wt, wv, strip, sb, rb, ext, rext, cext, hext, iext, flat, hs, edge_s, edge_r, spr_s, spr_r) = scr[:17]
    col_s, col_r, row_s, row_r, rcol_s, rcol_r, rrow_s, rrow_r = scr[17:25]
    im_sem, w_sem, a2a_send, a2a_recv = scr[25:29]
    sems = scr[29:]
    row = lax.axis_index("row")
    col = lax.axis_index("col")
    me = row * COLS + col

    im_copy = pltpu.make_async_copy(img_hbm, img, im_sem)
    im_copy.start()

    def there(axis, side):
        at, n = (row, ROWS) if axis == "row" else (col, COLS)
        return at < n - 1 if side else at > 0

    barrier = pltpu.get_barrier_semaphore()

    def greet(i, carry):
        tr = (row + i) & (ROWS - 1)
        for j in range(COLS):
            pl.semaphore_signal(
                barrier, inc=1, device_id=(tr, (col + j) & (COLS - 1)), device_id_type=MESH
            )
        return carry

    lax.fori_loop(1, ROWS, greet, 0)
    for j in range(1, COLS):
        pl.semaphore_signal(
            barrier, inc=1, device_id=(row, (col + j) & (COLS - 1)), device_id_type=MESH
        )

    w_copy = pltpu.make_async_copy(w_hbm, wt, w_sem)
    w_copy.start()

    im_copy.wait()
    pixels = img[...].reshape(CH * WIDTH, HEIGHT).astype(F32)
    count = CH * HEIGHT * WIDTH
    center = jnp.sum(pixels, axis=(0, 1), keepdims=True) / count
    shifted = pixels - center
    variance = jnp.sum(shifted * shifted, axis=(0, 1), keepdims=True) / count
    normed = (shifted / jnp.sqrt(variance + EPS)).astype(BF16)

    planes = jnp.concatenate([normed[c * WIDTH : (c + 1) * WIDTH] for c in range(CH)], axis=1)
    yy = lax.broadcasted_iota(jnp.int32, (HEIGHT, 128), 0)
    lane = lax.broadcasted_iota(jnp.int32, (HEIGHT, 128), 1)
    where_from = []
    for c in range(CH):
        offset = jnp.where((lane >> 5) == c, yy - 4 * (lane & 31), -1)
        where_from.append(
            jnp.concatenate([jnp.where(offset == j, 1.0, 0.0) for j in range(4)], axis=1)
        )
    spread_y = jnp.concatenate(where_from, axis=0).astype(BF16)
    strips = jnp.dot(planes, spread_y, preferred_element_type=F32)
    for j in range(4):
        strip[j, 0:8, :] = jnp.zeros((8, 128), F32)
        strip[j, 8 : 8 + WIDTH, :] = strips[:, j * 128 : j * 128 + 128]
        strip[j, 8 + WIDTH : 32 + WIDTH, :] = jnp.zeros((24, 128), F32)

    def cut(t, carry):
        parts = [strip[j, pl.ds(12 * t, 32), :] for j in range(4)]
        block = jnp.concatenate(parts, axis=0).astype(BF16).T
        view = sb.at[t].reshape(CH * 64, 128)
        for c in range(CH):
            view[c * 64 : c * 64 + 16, :] = jnp.zeros((16, 128), BF16)
            view[c * 64 + 16 : c * 64 + 48, :] = block[c * 32 : c * 32 + 32]
            view[c * 64 + 48 : c * 64 + 64, :] = jnp.zeros((16, 128), BF16)
        return carry

    lax.fori_loop(0, COLS, cut, 0)

    pl.semaphore_wait(barrier, DEVS - 1)

    own = pltpu.make_async_copy(
        sb.at[col, :, pl.ds(7 + 2 * row, 4)], rb.at[:, :, me], a2a_recv
    )
    own.start()

    def send_block(tr, tc):
        pltpu.make_async_remote_copy(
            src_ref=sb.at[tc, :, pl.ds(7 + 2 * tr, 4)],
            dst_ref=rb.at[:, :, me],
            send_sem=a2a_send,
            recv_sem=a2a_recv,
            device_id=(tr, tc),
            device_id_type=MESH,
        ).start()

    def send_row(i, carry):
        tr = (row + i) & (ROWS - 1)
        for j in range(COLS):
            send_block(tr, (col + j) & (COLS - 1))
        return carry

    lax.fori_loop(1, ROWS, send_row, 0)
    for j in range(1, COLS):
        send_block(row, (col + j) & (COLS - 1))

    for side in SIDES:

        @pl.when(jnp.logical_not(there("col", side)))
        def _(side=side):
            for p in range(PR):
                hext[p, 4 * side] = jnp.zeros((F, B), BF16)
                iext[p, 4 * side] = jnp.zeros((F, B), BF16)
            for ref in (col_r, rcol_r):
                ref[side] = jnp.zeros(ref.shape[1:], BF16)

        @pl.when(jnp.logical_not(there("row", side)))
        def _(side=side):
            for ref in (edge_r, spr_r, row_r, rrow_r):
                ref[side] = jnp.zeros(ref.shape[1:], BF16)

    cext[...] = jnp.zeros(cext.shape, F32)
    w_copy.wait()

    def flip(pos, carry):
        for kb in range(0, K, 128):
            n = min(128, K - kb)
            wv[pos, :, kb : kb + n] = wt[pos, kb : kb + n, :].T
        return carry

    lax.fori_loop(0, PR * PC, flip, 0)

    mr = lax.broadcasted_iota(jnp.int32, (256, 256), 0)
    mc = lax.broadcasted_iota(jnp.int32, (256, 256), 1)
    split = jnp.where(
        mr == jnp.where(mc < 128, 2 * mc, 2 * mc - 255), 1.0, 0.0
    ).astype(BF16)

    pltpu.make_async_copy(rb, rb, a2a_recv).wait()

    for c in range(CH):
        for i in range(4):
            pair = rb.at[c, i].reshape(256, 128)[...]
            turned = lax.dot_general(
                pair, split, (((0,), (0,)), ((), ())), preferred_element_type=F32
            )
            for par in range(2):
                y0 = 8 * i + 4 * par
                ext[c, y0 : y0 + 4, 8:40, :] = turned[:, par * 128 : par * 128 + 128].reshape(4, 32, 128)

    low = lax.broadcasted_iota(jnp.int32, (8, 128), 0) < 4

    def patch(src, p, x0):
        blocks = []
        for c in range(CH):
            for u in range(0, FIELD, 2):
                y = S * p + u
                blocks += [
                    src[c, y, pl.ds(x0, 8), :],
                    src[c, y, pl.ds(x0 + 8, 8), :],
                    jnp.where(low, src[c, y, pl.ds(x0 + 16, 8), :], src[c, y + 1, pl.ds(x0 - 4, 8), :]),
                    src[c, y + 1, pl.ds(x0 + 4, 8), :],
                    src[c, y + 1, pl.ds(x0 + 12, 8), :],
                ]
        return jnp.concatenate(blocks, axis=0).astype(BF16)

    def unpatch(dst, terms, p, x0):
        blocks = [terms[8 * m : 8 * m + 8] for m in range(K // 8)]
        for c in range(CH):
            for u in range(0, FIELD, 2):
                y = S * p + u
                b0, b1, b2, b3, b4 = blocks[(c * FIELD + u) // 2 * 5 :][:5]
                dst[c, y, pl.ds(x0, 8), :] += b0
                dst[c, y, pl.ds(x0 + 8, 8), :] += b1
                dst[c, y, pl.ds(x0 + 16, 8), :] += jnp.where(low, b2, 0.0)
                dst[c, y + 1, pl.ds(x0 - 4, 8), :] += jnp.where(low, 0.0, b2)
                dst[c, y + 1, pl.ds(x0 + 4, 8), :] += b3
                dst[c, y + 1, pl.ds(x0 + 12, 8), :] += b4

    def encode(p, carry):
        zero = lax.shift_right_logical(p, 4)
        for q in range(PC):
            pos = PC * p + q
            columns = patch(ext, p, zero + (8 + S * q))
            pat[pos] = columns
            hidden = jnp.dot(wv[pos], columns, preferred_element_type=F32).astype(BF16)
            hext[p, q + 1] = hidden
            hid_out[pos] = hidden
        return carry

    lax.fori_loop(0, PR, encode, 0)

    class Exchange:
        def __init__(self, n, axis, src, dst):
            self.axis, self.src, self.dst = axis, src, dst
            self.send, self.recv = sems[2 * n], sems[2 * n + 1]

        def copy(self, side):
            step = 1 if side else -1
            to = (row + step, col) if self.axis == "row" else (row, col + step)
            return pltpu.make_async_remote_copy(
                src_ref=self.src(side),
                dst_ref=self.dst(1 - side),
                send_sem=self.send.at[side],
                recv_sem=self.recv.at[side],
                device_id=to,
                device_id_type=MESH,
            )

        def each(self, act):
            for side in SIDES:

                @pl.when(there(self.axis, side))
                def _(side=side):
                    act(side)

        def start(self):
            self.each(lambda side: self.copy(side).start())

        def arrive(self):
            self.each(lambda side: self.copy(1 - side).wait_recv())

        def sent(self):
            self.each(lambda side: self.copy(side).wait_send())

    def side_columns(ref):
        return (
            lambda side: ref.at[:, 3 if side else 1],
            lambda side: ref.at[:, 4 if side else 0],
        )

    def whole(send, recv):
        return lambda side: send.at[side], lambda side: recv.at[side]

    hidden_x = Exchange(0, "col", *side_columns(hext))
    square_x = Exchange(1, "row", *whole(edge_s, edge_r))
    inverse_x = Exchange(2, "col", *side_columns(iext))
    spread_x = Exchange(3, "row", *whole(spr_s, spr_r))
    terms_cx = Exchange(4, "col", *whole(col_s, col_r))
    terms_rx = Exchange(5, "row", *whole(row_s, row_r))
    resid_rx = Exchange(6, "row", *whole(rrow_s, rrow_r))
    resid_cx = Exchange(7, "col", *whole(rcol_s, rcol_r))

    hidden_x.start()

    def decode(p, carry):
        zero = lax.shift_right_logical(p, 4)
        for q in range(PC):
            pos = PC * p + q
            terms = jnp.dot(wt[pos], hid_out[pos], preferred_element_type=F32)
            unpatch(cext, terms, p, zero + (8 + S * q))
        return carry

    lax.fori_loop(0, PR, decode, 0)

    zero = lax.shift_right_logical(row, 8)

    def pack_rows(src, y0):
        blocks = []
        for c in range(CH):
            for y in range(y0, y0 + 8, 2):
                blocks += [
                    src[c, y, pl.ds(zero + 16, 8), :],
                    jnp.where(low, src[c, y, pl.ds(zero + 24, 8), :], src[c, y + 1, pl.ds(zero + 12, 8), :]),
                    src[c, y + 1, pl.ds(zero + 20, 8), :],
                ]
        return jnp.concatenate(blocks, axis=0).astype(BF16)

    def unpack_rows(got, y0):
        for c in range(CH):
            for n in range(4):
                at = (c * 4 + n) * 24
                yield c, y0 + 2 * n, [got[at + 8 * m : at + 8 * m + 8] for m in range(3)]

    def columns_of(src, x):
        return src[:, :, pl.ds(zero + x, 8), :].reshape(CH * 32 * 8, 128).astype(BF16)

    for side in SIDES:
        col_s[side] = columns_of(cext, OUTER[side])
    terms_cx.start()

    hidden_x.arrive()

    def across(get):
        cells = [get(b) for b in range(PC + 2)]
        return [cells[b] + cells[b + 1] + cells[b + 2] for b in range(PC)]

    def chunk(n):
        return pl.ds(pl.multiple_of(n * 16, 16), 16)

    def squares(n, carry):
        rows16 = chunk(n)
        for p in range(PR):

            def square(b):
                v = hext[p, b, rows16, :].astype(F32)
                return v * v

            for q, total in enumerate(across(square)):
                flat[p, q, rows16, :] = total
                if p == 0:
                    edge_s[0, q, rows16, :] = total.astype(BF16)
                if p == PR - 1:
                    edge_s[1, q, rows16, :] = total.astype(BF16)
        return carry

    lax.fori_loop(0, F // 16, squares, 0)
    square_x.start()

    terms_cx.arrive()
    for side in SIDES:
        cext[:, :, pl.ds(zero + INNER[side], 8), :] += (
            col_r[side].astype(F32).reshape(CH, 32, 8, 128)
        )
    for side in SIDES:
        row_s[side] = pack_rows(cext, TOP[side])
    terms_rx.start()

    square_x.arrive()

    def down(q, rows16, outside):
        cells = [outside[0, q, rows16, :].astype(F32)]
        cells += [flat[p, q, rows16, :] for p in range(PR)]
        cells += [outside[1, q, rows16, :].astype(F32)]
        return [cells[p] + cells[p + 1] + cells[p + 2] for p in range(PR)]

    def pool(n, carry):
        rows16 = chunk(n)
        for q in range(PC):
            for p, total in enumerate(down(q, rows16, edge_r)):
                energy = jnp.sqrt(1.0 + total)
                iext[p, q + 1, rows16, :] = (1.0 / energy).astype(BF16)
        return carry

    lax.fori_loop(0, F // 16, pool, 0)
    inverse_x.start()

    terms_rx.arrive()
    for side in SIDES:
        got = row_r[side].astype(F32)
        for c, y, (b0, b1, b2) in unpack_rows(got, EDGE[side]):
            cext[c, y, pl.ds(zero + 16, 8), :] += b0
            cext[c, y, pl.ds(zero + 24, 8), :] += jnp.where(low, b1, 0.0)
            cext[c, y + 1, pl.ds(zero + 12, 8), :] += jnp.where(low, 0.0, b1)
            cext[c, y + 1, pl.ds(zero + 20, 8), :] += b2
    for x, n in ((16, 8), (24, 4)):
        at = slice(x, x + n)
        resid = cext[:, 8:24, at, :] - ext[:, 8:24, at, :]
        rext[:, 8:24, at, :] = resid.astype(BF16).astype(F32)
    for side in SIDES:
        rrow_s[side] = pack_rows(rext, EDGE[side])
    resid_rx.start()

    inverse_x.arrive()

    def inverses(n, carry):
        rows16 = chunk(n)
        for p in range(PR):
            for q, total in enumerate(across(lambda b: iext[p, b, rows16, :].astype(F32))):
                flat[p, q, rows16, :] = total
                if p == 0:
                    spr_s[0, q, rows16, :] = total.astype(BF16)
                if p == PR - 1:
                    spr_s[1, q, rows16, :] = total.astype(BF16)
        return carry

    lax.fori_loop(0, F // 16, inverses, 0)
    spread_x.start()

    resid_rx.arrive()
    for side in SIDES:
        got = rrow_r[side].astype(F32)
        for c, y, (b0, b1, b2) in unpack_rows(got, TOP[side]):
            rext[c, y, pl.ds(zero + 16, 8), :] = b0
            rext[c, y, pl.ds(zero + 24, 8), :] = b1
            rext[c, y + 1, pl.ds(zero + 12, 8), :] = b1
            rext[c, y + 1, pl.ds(zero + 20, 8), :] = b2
    for side in SIDES:
        rcol_s[side] = columns_of(rext, INNER[side])
    resid_cx.start()

    spread_x.arrive()

    def widen(n, carry):
        rows16 = chunk(n)
        for q in range(PC):
            for p, total in enumerate(down(q, rows16, spr_r)):
                hidden = hid_out[p * PC + q, rows16, :].astype(F32)
                hs[p * PC + q, rows16, :] = SPARSITY * hidden * total
        return carry

    lax.fori_loop(0, F // 16, widen, 0)

    resid_cx.arrive()
    for side in SIDES:
        rext[:, :, pl.ds(zero + OUTER[side], 8), :] = (
            rcol_r[side].astype(F32).reshape(CH, 32, 8, 128)
        )

    def backward(p, carry):
        zero = lax.shift_right_logical(p, 4)
        for q in range(PC):
            pos = PC * p + q
            columns = patch(rext, p, zero + (8 + S * q))
            rpat[pos] = columns
            back = hs[pos] + jnp.dot(wv[pos], columns, preferred_element_type=F32)
            back_out[pos] = back.astype(BF16)
        return carry

    lax.fori_loop(0, PR, backward, 0)

    pltpu.make_async_copy(
        rb.at[:, :, pl.ds(0, DEVS - 1)], rb.at[:, :, pl.ds(0, DEVS - 1)], a2a_send
    ).wait()
    for exchange in (hidden_x, square_x, inverse_x, spread_x, terms_cx, terms_rx, resid_rx, resid_cx):
        exchange.sent()


def grad_kernel(pat, rpat, back, hid, out, stage, sems):
    halves = (slice(0, K // 2), slice(K // 2, K))
    copies = []
    for pos in range(PR * PC):
        right = jnp.concatenate([back[pos], hid[pos]], axis=1)
        for n, rows in enumerate(halves):
            left = jnp.concatenate([pat[pos, rows, :], rpat[pos, rows, :]], axis=1)
            grad = lax.dot_general(left, right, (((1,), (1,)), ((), ())), preferred_element_type=F32)
            stage[pos, rows, :] = grad * (1.0 / B)
            copy = pltpu.make_async_copy(stage.at[pos, rows], out.at[pos, rows], sems.at[pos, n])
            copy.start()
            copies.append(copy)
    for copy in copies:
        copy.wait()


def main_call(images, weights):
    dma = pltpu.SemaphoreType.DMA
    vmem = pl.BlockSpec(memory_space=pltpu.VMEM)
    hbm = pl.BlockSpec(memory_space=pltpu.HBM)
    n_pos = PR * PC
    return pl.pallas_call(
        main_kernel,
        name="rica_main",
        out_shape=(
            pltpu.VMEM((n_pos, K, B), BF16),
            pltpu.VMEM((n_pos, K, B), BF16),
            pltpu.VMEM((n_pos, F, B), BF16),
            pltpu.VMEM((n_pos, F, B), BF16),
        ),
        in_specs=[hbm, hbm],
        out_specs=(vmem, vmem, vmem, vmem),
        scratch_shapes=[
            pltpu.VMEM((CH, WIDTH, HEIGHT), BF16),
            pltpu.VMEM((n_pos, K, F), BF16),
            pltpu.VMEM((n_pos, F, K), BF16),
            pltpu.VMEM((4, WIDTH + 32, 128), F32),
            pltpu.VMEM((COLS, CH, 32, 2, 128), BF16),
            pltpu.VMEM((CH, 4, DEVS, 2, 128), BF16),
            pltpu.VMEM((CH, 32, 40, 128), F32),
            pltpu.VMEM((CH, 32, 40, 128), F32),
            pltpu.VMEM((CH, 32, 40, 128), F32),
            pltpu.VMEM((PR, PC + 2, F, B), BF16),
            pltpu.VMEM((PR, PC + 2, F, B), BF16),
            pltpu.VMEM((PR, PC, F, B), F32),
            pltpu.VMEM((n_pos, F, B), F32),
            *[pltpu.VMEM((2, PC, F, B), BF16) for _ in range(4)],
            *[pltpu.VMEM((2, CH * 32 * 8, 128), BF16) for _ in range(2)],
            *[pltpu.VMEM((2, CH * 8 * 12, 128), BF16) for _ in range(2)],
            *[pltpu.VMEM((2, CH * 32 * 8, 128), BF16) for _ in range(2)],
            *[pltpu.VMEM((2, CH * 8 * 12, 128), BF16) for _ in range(2)],
            *[dma for _ in range(4)],
            *[dma((2,)) for _ in range(16)],
        ],
        compiler_params=pltpu.CompilerParams(
            collective_id=0, has_side_effects=True, vmem_limit_bytes=36 * 1024 * 1024
        ),
    )(images, weights)


def grad_call(*factors):
    n_pos = PR * PC
    vmem = pl.BlockSpec(memory_space=pltpu.VMEM)
    return pl.pallas_call(
        grad_kernel,
        name="rica_grad",
        out_shape=jax.ShapeDtypeStruct((n_pos, K, F), F32),
        in_specs=[vmem] * 4,
        out_specs=pl.BlockSpec(memory_space=pltpu.HBM),
        scratch_shapes=[
            pltpu.VMEM((n_pos, K, F), F32),
            pltpu.SemaphoreType.DMA((n_pos, 2)),
        ],
        compiler_params=pltpu.CompilerParams(vmem_limit_bytes=12 * 1024 * 1024),
    )(*factors)


def body(images, weights):
    images = images.reshape(CH, HEIGHT, WIDTH).transpose(0, 2, 1)
    weights = weights.reshape(PR * PC, F, K).transpose(0, 2, 1)
    images = pltpu.with_memory_space_constraint(images, pltpu.HBM)
    weights = pltpu.with_memory_space_constraint(weights, pltpu.HBM)
    factors = main_call(images, weights)
    factors = [pltpu.with_memory_space_constraint(x, pltpu.VMEM) for x in factors]
    grad = grad_call(*factors)
    return grad.transpose(0, 2, 1).reshape(PR, PC, F, K)


def solution(mesh):
    return jax.shard_map(
        body,
        mesh=mesh,
        in_specs=(P(("row", "col"), None, None, None), P("row", "col", None, None)),
        out_specs=P("row", "col", None, None),
        check_vma=False,
    )
```

```python
import jax
import jax.numpy as jnp
from jax import lax
from jax.experimental import pallas as pl
from jax.experimental.pallas import tpu as pltpu
from jax.sharding import PartitionSpec as P

MESH = pl.DeviceIdType.MESH
F32 = jnp.float32
BF16 = jnp.bfloat16

ROWS, COLS = 8, 16
DEVS = ROWS * COLS
CH, S, FIELD, PAD = 3, 4, 20, 8
K = 1200
F = 128
B = 128
HEIGHT, WIDTH = 128, 192
PR, PC = 4, 3
SPARSITY = 0.5
EPS = 1e-05

SIDES = (0, 1)
DIRS = [(dr, dc) for dr in (-1, 0, 1) for dc in (-1, 0, 1) if (dr, dc) != (0, 0)]
OUTER_Y, OUTER_X = {-1: 0, 0: 8, 1: 24}, {-1: 8, 1: 28}
INNER_Y, INNER_X = {-1: 8, 0: 8, 1: 16}, {-1: 16, 1: 20}
RIM = [CH * (288 // CH if dc == 0 else 8 * (16 if dr == 0 else 8)) for dr, dc in DIRS]


def low_rows():
    return lax.broadcasted_iota(jnp.int32, (8, 128), 0) < 4


def patch(src, p, x0):
    low = low_rows()
    blocks = []
    for c in range(CH):
        for u in range(0, FIELD, 2):
            y = S * p + u
            blocks += [
                src[c, y, pl.ds(x0, 8), :],
                src[c, y, pl.ds(x0 + 8, 8), :],
                jnp.where(low, src[c, y, pl.ds(x0 + 16, 8), :], src[c, y + 1, pl.ds(x0 - 4, 8), :]),
                src[c, y + 1, pl.ds(x0 + 4, 8), :],
                src[c, y + 1, pl.ds(x0 + 12, 8), :],
            ]
    return jnp.concatenate(blocks, axis=0).astype(BF16)


def main_kernel(img_hbm, w_hbm, pat, wv, rext, hs, hid_out, *scr):
    (img, wt, strip, sb, rb, ext, cext, hext, iext, flat, edge_s, edge_r, spr_s, spr_r) = scr[:14]
    terms_s, terms_r, resid_s, resid_r = scr[14:22], scr[22:30], scr[30:38], scr[38:46]
    im_sem, w_sem, a2a_send, a2a_recv = scr[46:50]
    sems = scr[50:]
    row = lax.axis_index("row")
    col = lax.axis_index("col")
    me = row * COLS + col

    im_copy = pltpu.make_async_copy(img_hbm, img, im_sem)
    im_copy.start()

    def there(axis, side):
        at, n = (row, ROWS) if axis == "row" else (col, COLS)
        return at < n - 1 if side else at > 0

    barrier = pltpu.get_barrier_semaphore()

    def greet(i, carry):
        tr = (row + i) & (ROWS - 1)
        for j in range(COLS):
            pl.semaphore_signal(
                barrier, inc=1, device_id=(tr, (col + j) & (COLS - 1)), device_id_type=MESH
            )
        return carry

    lax.fori_loop(1, ROWS, greet, 0)
    for j in range(1, COLS):
        pl.semaphore_signal(
            barrier, inc=1, device_id=(row, (col + j) & (COLS - 1)), device_id_type=MESH
        )

    w_copy = pltpu.make_async_copy(w_hbm, wt, w_sem)
    w_copy.start()

    im_copy.wait()
    pixels = img[...].reshape(CH * WIDTH, HEIGHT).astype(F32)
    count = CH * HEIGHT * WIDTH
    center = jnp.sum(pixels, axis=(0, 1), keepdims=True) / count
    shifted = pixels - center
    variance = jnp.sum(shifted * shifted, axis=(0, 1), keepdims=True) / count
    normed = (shifted / jnp.sqrt(variance + EPS)).astype(BF16)

    planes = jnp.concatenate([normed[c * WIDTH : (c + 1) * WIDTH] for c in range(CH)], axis=1)
    yy = lax.broadcasted_iota(jnp.int32, (HEIGHT, 128), 0)
    lane = lax.broadcasted_iota(jnp.int32, (HEIGHT, 128), 1)
    where_from = []
    for c in range(CH):
        offset = jnp.where((lane >> 5) == c, yy - 4 * (lane & 31), -1)
        where_from.append(
            jnp.concatenate([jnp.where(offset == j, 1.0, 0.0) for j in range(4)], axis=1)
        )
    spread_y = jnp.concatenate(where_from, axis=0).astype(BF16)
    strips = jnp.dot(planes, spread_y, preferred_element_type=F32)
    for j in range(4):
        strip[j, 0:8, :] = jnp.zeros((8, 128), F32)
        strip[j, 8 : 8 + WIDTH, :] = strips[:, j * 128 : j * 128 + 128]
        strip[j, 8 + WIDTH : 32 + WIDTH, :] = jnp.zeros((24, 128), F32)

    def cut(t, carry):
        parts = [strip[j, pl.ds(12 * t, 32), :] for j in range(4)]
        block = jnp.concatenate(parts, axis=0).astype(BF16).T
        view = sb.at[t].reshape(CH * 64, 128)
        for c in range(CH):
            view[c * 64 : c * 64 + 16, :] = jnp.zeros((16, 128), BF16)
            view[c * 64 + 16 : c * 64 + 48, :] = block[c * 32 : c * 32 + 32]
            view[c * 64 + 48 : c * 64 + 64, :] = jnp.zeros((16, 128), BF16)
        return carry

    lax.fori_loop(0, COLS, cut, 0)

    pl.semaphore_wait(barrier, DEVS - 1)

    own = pltpu.make_async_copy(
        sb.at[col, :, pl.ds(7 + 2 * row, 4)], rb.at[:, :, me], a2a_recv
    )
    own.start()

    def send_block(tr, tc):
        pltpu.make_async_remote_copy(
            src_ref=sb.at[tc, :, pl.ds(7 + 2 * tr, 4)],
            dst_ref=rb.at[:, :, me],
            send_sem=a2a_send,
            recv_sem=a2a_recv,
            device_id=(tr, tc),
            device_id_type=MESH,
        ).start()

    def send_row(i, carry):
        tr = (row + i) & (ROWS - 1)
        for j in range(COLS):
            send_block(tr, (col + j) & (COLS - 1))
        return carry

    lax.fori_loop(1, ROWS, send_row, 0)
    for j in range(1, COLS):
        send_block(row, (col + j) & (COLS - 1))

    for side in SIDES:

        @pl.when(jnp.logical_not(there("col", side)))
        def _(side=side):
            for p in range(PR):
                hext[p, 4 * side] = jnp.zeros((F, B), BF16)
                iext[p, 4 * side] = jnp.zeros((F, B), BF16)

        @pl.when(jnp.logical_not(there("row", side)))
        def _(side=side):
            for ref in (edge_r, spr_r):
                ref[side] = jnp.zeros(ref.shape[1:], BF16)

    def near(k):
        dr, dc = DIRS[k]
        ok = None
        for axis, d in (("row", dr), ("col", dc)):
            if d:
                one = there(axis, (d + 1) // 2)
                ok = one if ok is None else ok & one
        return ok

    for k in range(8):

        @pl.when(jnp.logical_not(near(k)))
        def _(k=k):
            for ref in (terms_r[k], resid_r[k]):
                ref[...] = jnp.zeros(ref.shape, BF16)

    cext[...] = jnp.zeros(cext.shape, F32)
    w_copy.wait()

    def flip(pos, carry):
        for kb in range(0, K, 128):
            n = min(128, K - kb)
            wv[pos, :, kb : kb + n] = wt[pos, kb : kb + n, :].T
        return carry

    lax.fori_loop(0, PR * PC, flip, 0)

    mr = lax.broadcasted_iota(jnp.int32, (256, 256), 0)
    mc = lax.broadcasted_iota(jnp.int32, (256, 256), 1)
    split = jnp.where(
        mr == jnp.where(mc < 128, 2 * mc, 2 * mc - 255), 1.0, 0.0
    ).astype(BF16)

    pltpu.make_async_copy(rb, rb, a2a_recv).wait()

    for c in range(CH):
        for i in range(4):
            pair = rb.at[c, i].reshape(256, 128)[...]
            turned = lax.dot_general(
                pair, split, (((0,), (0,)), ((), ())), preferred_element_type=F32
            )
            for par in range(2):
                y0 = 8 * i + 4 * par
                ext[c, y0 : y0 + 4, 8:40, :] = turned[:, par * 128 : par * 128 + 128].reshape(4, 32, 128)

    low = low_rows()

    def unpatch(dst, terms, p, x0):
        blocks = [terms[8 * m : 8 * m + 8] for m in range(K // 8)]
        for c in range(CH):
            for u in range(0, FIELD, 2):
                y = S * p + u
                b0, b1, b2, b3, b4 = blocks[(c * FIELD + u) // 2 * 5 :][:5]
                dst[c, y, pl.ds(x0, 8), :] += b0
                dst[c, y, pl.ds(x0 + 8, 8), :] += b1
                dst[c, y, pl.ds(x0 + 16, 8), :] += jnp.where(low, b2, 0.0)
                dst[c, y + 1, pl.ds(x0 - 4, 8), :] += jnp.where(low, 0.0, b2)
                dst[c, y + 1, pl.ds(x0 + 4, 8), :] += b3
                dst[c, y + 1, pl.ds(x0 + 12, 8), :] += b4

    def encode(p, carry):
        zero = lax.shift_right_logical(p, 4)
        for q in range(PC):
            pos = PC * p + q
            columns = patch(ext, p, zero + (8 + S * q))
            pat[pos] = columns
            hidden = jnp.dot(wv[pos], columns, preferred_element_type=F32).astype(BF16)
            hext[p, q + 1] = hidden
            hid_out[pos] = hidden
        return carry

    lax.fori_loop(0, PR, encode, 0)

    class Exchange:
        def __init__(self, n, axis, src, dst):
            self.axis, self.src, self.dst = axis, src, dst
            self.send, self.recv = sems[2 * n], sems[2 * n + 1]

        def copy(self, side):
            step = 1 if side else -1
            to = (row + step, col) if self.axis == "row" else (row, col + step)
            return pltpu.make_async_remote_copy(
                src_ref=self.src(side),
                dst_ref=self.dst(1 - side),
                send_sem=self.send.at[side],
                recv_sem=self.recv.at[side],
                device_id=to,
                device_id_type=MESH,
            )

        def each(self, act):
            for side in SIDES:

                @pl.when(there(self.axis, side))
                def _(side=side):
                    act(side)

        def start(self):
            self.each(lambda side: self.copy(side).start())

        def arrive(self):
            self.each(lambda side: self.copy(1 - side).wait_recv())

        def sent(self):
            self.each(lambda side: self.copy(side).wait_send())

    def side_columns(ref):
        return (
            lambda side: ref.at[:, 3 if side else 1],
            lambda side: ref.at[:, 4 if side else 0],
        )

    def whole(send, recv):
        return lambda side: send.at[side], lambda side: recv.at[side]

    hidden_x = Exchange(0, "col", *side_columns(hext))
    square_x = Exchange(1, "row", *whole(edge_s, edge_r))
    inverse_x = Exchange(2, "col", *side_columns(iext))
    spread_x = Exchange(3, "row", *whole(spr_s, spr_r))

    class Around:
        def __init__(self, n, send, recv):
            self.bufs, self.sems = (send, recv), (sems[n], sems[n + 1])

        def copy(self, k):
            dr, dc = DIRS[k]
            return pltpu.make_async_remote_copy(
                src_ref=self.bufs[0][k],
                dst_ref=self.bufs[1][7 - k],
                send_sem=self.sems[0].at[k],
                recv_sem=self.sems[1].at[7 - k],
                device_id=(row + dr, col + dc),
                device_id_type=MESH,
            )

        def each(self, act):
            for k in range(8):

                @pl.when(near(k))
                def _(k=k):
                    act(k)

        def start(self):
            self.each(lambda k: self.copy(k).start())

        def arrive(self):
            self.each(lambda k: self.copy(7 - k).wait_recv())

        def sent(self):
            self.each(lambda k: self.copy(k).wait_send())

    terms_x = Around(8, terms_s, terms_r)
    resid_x = Around(10, resid_s, resid_r)

    hidden_x.start()

    def decode(p, carry):
        zero = lax.shift_right_logical(p, 4)
        for q in range(PC):
            pos = PC * p + q
            terms = jnp.dot(wt[pos], hid_out[pos], preferred_element_type=F32)
            unpatch(cext, terms, p, zero + (8 + S * q))
        return carry

    lax.fori_loop(0, PR, decode, 0)

    zero = lax.shift_right_logical(row, 8)

    def pack_rows(src, y0):
        blocks = []
        for c in range(CH):
            for y in range(y0, y0 + 8, 2):
                blocks += [
                    src[c, y, pl.ds(zero + 16, 8), :],
                    jnp.where(low, src[c, y, pl.ds(zero + 24, 8), :], src[c, y + 1, pl.ds(zero + 12, 8), :]),
                    src[c, y + 1, pl.ds(zero + 20, 8), :],
                ]
        return jnp.concatenate(blocks, axis=0).astype(BF16)

    def unpack_rows(got, y0):
        for c in range(CH):
            for n in range(4):
                at = (c * 4 + n) * 24
                yield c, y0 + 2 * n, [got[at + 8 * m : at + 8 * m + 8] for m in range(3)]

    def pack(src, k, ys, xs):
        dr, dc = DIRS[k]
        if dc == 0:
            return pack_rows(src, ys[dr])
        ny = 16 if dr == 0 else 8
        part = src[:, ys[dr] : ys[dr] + ny, pl.ds(zero + xs[dc], 8), :]
        return part.reshape(RIM[k], 128).astype(BF16)

    for k in range(8):
        terms_s[k][...] = pack(cext, k, OUTER_Y, OUTER_X)
    terms_x.start()

    hidden_x.arrive()

    def across(get):
        cells = [get(b) for b in range(PC + 2)]
        return [cells[b] + cells[b + 1] + cells[b + 2] for b in range(PC)]

    def chunk(n):
        return pl.ds(pl.multiple_of(n * 16, 16), 16)

    def squares(n, carry):
        rows16 = chunk(n)
        for p in range(PR):

            def square(b):
                v = hext[p, b, rows16, :].astype(F32)
                return v * v

            for q, total in enumerate(across(square)):
                flat[p, q, rows16, :] = total
                if p == 0:
                    edge_s[0, q, rows16, :] = total.astype(BF16)
                if p == PR - 1:
                    edge_s[1, q, rows16, :] = total.astype(BF16)
        return carry

    lax.fori_loop(0, F // 16, squares, 0)
    square_x.start()

    square_x.arrive()

    def down(q, rows16, outside):
        cells = [outside[0, q, rows16, :].astype(F32)]
        cells += [flat[p, q, rows16, :] for p in range(PR)]
        cells += [outside[1, q, rows16, :].astype(F32)]
        return [cells[p] + cells[p + 1] + cells[p + 2] for p in range(PR)]

    def pool(n, carry):
        rows16 = chunk(n)
        for q in range(PC):
            for p, total in enumerate(down(q, rows16, edge_r)):
                energy = jnp.sqrt(1.0 + total)
                iext[p, q + 1, rows16, :] = (1.0 / energy).astype(BF16)
        return carry

    lax.fori_loop(0, F // 16, pool, 0)
    inverse_x.start()

    terms_x.arrive()
    for k, (dr, dc) in enumerate(DIRS):
        got = terms_r[k][...].astype(F32)
        if dc == 0:
            for c, y, (b0, b1, b2) in unpack_rows(got, INNER_Y[dr]):
                cext[c, y, pl.ds(zero + 16, 8), :] += b0
                cext[c, y, pl.ds(zero + 24, 8), :] += jnp.where(low, b1, 0.0)
                cext[c, y + 1, pl.ds(zero + 12, 8), :] += jnp.where(low, 0.0, b1)
                cext[c, y + 1, pl.ds(zero + 20, 8), :] += b2
        else:
            ny = 16 if dr == 0 else 8
            y0 = INNER_Y[dr]
            cext[:, y0 : y0 + ny, pl.ds(zero + INNER_X[dc], 8), :] += got.reshape(CH, ny, 8, 128)
    for x, n in ((16, 8), (24, 4)):
        at = slice(x, x + n)
        resid = cext[:, 8:24, at, :] - ext[:, 8:24, at, :]
        rext[:, 8:24, at, :] = resid.astype(BF16).astype(F32)
    for k in range(8):
        resid_s[k][...] = pack(rext, k, INNER_Y, INNER_X)
    resid_x.start()

    inverse_x.arrive()

    def inverses(n, carry):
        rows16 = chunk(n)
        for p in range(PR):
            for q, total in enumerate(across(lambda b: iext[p, b, rows16, :].astype(F32))):
                flat[p, q, rows16, :] = total
                if p == 0:
                    spr_s[0, q, rows16, :] = total.astype(BF16)
                if p == PR - 1:
                    spr_s[1, q, rows16, :] = total.astype(BF16)
        return carry

    lax.fori_loop(0, F // 16, inverses, 0)
    spread_x.start()

    spread_x.arrive()

    def widen(n, carry):
        rows16 = chunk(n)
        for q in range(PC):
            for p, total in enumerate(down(q, rows16, spr_r)):
                hidden = hid_out[p * PC + q, rows16, :].astype(F32)
                hs[p * PC + q, rows16, :] = SPARSITY * hidden * total
        return carry

    lax.fori_loop(0, F // 16, widen, 0)

    resid_x.arrive()
    for k in sorted(range(8), key=lambda k: DIRS[k][1] != 0):
        dr, dc = DIRS[k]
        got = resid_r[k][...].astype(F32)
        if dc == 0:
            for c, y, (b0, b1, b2) in unpack_rows(got, OUTER_Y[dr]):
                rext[c, y, pl.ds(zero + 16, 8), :] = b0
                rext[c, y, pl.ds(zero + 24, 8), :] = b1
                rext[c, y + 1, pl.ds(zero + 12, 8), :] = b1
                rext[c, y + 1, pl.ds(zero + 20, 8), :] = b2
        else:
            ny = 16 if dr == 0 else 8
            y0 = OUTER_Y[dr]
            rext[:, y0 : y0 + ny, pl.ds(zero + OUTER_X[dc], 8), :] = got.reshape(CH, ny, 8, 128)

    pltpu.make_async_copy(
        rb.at[:, :, pl.ds(0, DEVS - 1)], rb.at[:, :, pl.ds(0, DEVS - 1)], a2a_send
    ).wait()
    for exchange in (hidden_x, square_x, inverse_x, spread_x, terms_x, resid_x):
        exchange.sent()


def grad_kernel(pat, wv, rext, hs, hid, out, stage, sems):
    halves = (slice(0, K // 2), slice(K // 2, K))
    copies = []
    zero = lax.shift_right_logical(lax.axis_index("row"), 8)
    for pos in range(PR * PC):
        p, q = divmod(pos, PC)
        columns = patch(rext, p, zero + (8 + S * q))
        back = hs[pos] + jnp.dot(wv[pos], columns, preferred_element_type=F32)
        right = jnp.concatenate([back.astype(BF16), hid[pos]], axis=1)
        for n, rows in enumerate(halves):
            left = jnp.concatenate([pat[pos, rows, :], columns[rows]], axis=1)
            grad = lax.dot_general(left, right, (((1,), (1,)), ((), ())), preferred_element_type=F32)
            stage[pos, rows, :] = grad * (1.0 / B)
            copy = pltpu.make_async_copy(stage.at[pos, rows], out.at[pos, rows], sems.at[pos, n])
            copy.start()
            copies.append(copy)
    for copy in copies:
        copy.wait()


def main_call(images, weights):
    dma = pltpu.SemaphoreType.DMA
    vmem = pl.BlockSpec(memory_space=pltpu.VMEM)
    hbm = pl.BlockSpec(memory_space=pltpu.HBM)
    n_pos = PR * PC
    return pl.pallas_call(
        main_kernel,
        name="rica_main",
        out_shape=(
            pltpu.VMEM((n_pos, K, B), BF16),
            pltpu.VMEM((n_pos, F, K), BF16),
            pltpu.VMEM((CH, 32, 40, 128), F32),
            pltpu.VMEM((n_pos, F, B), F32),
            pltpu.VMEM((n_pos, F, B), BF16),
        ),
        in_specs=[hbm, hbm],
        out_specs=(vmem,) * 5,
        scratch_shapes=[
            pltpu.VMEM((CH, WIDTH, HEIGHT), BF16),
            pltpu.VMEM((n_pos, K, F), BF16),
            pltpu.VMEM((4, WIDTH + 32, 128), F32),
            pltpu.VMEM((COLS, CH, 32, 2, 128), BF16),
            pltpu.VMEM((CH, 4, DEVS, 2, 128), BF16),
            pltpu.VMEM((CH, 32, 40, 128), F32),
            pltpu.VMEM((CH, 32, 40, 128), F32),
            pltpu.VMEM((PR, PC + 2, F, B), BF16),
            pltpu.VMEM((PR, PC + 2, F, B), BF16),
            pltpu.VMEM((PR, PC, F, B), F32),
            *[pltpu.VMEM((2, PC, F, B), BF16) for _ in range(4)],
            *[pltpu.VMEM((n, 128), BF16) for _ in range(4) for n in RIM],
            *[dma for _ in range(4)],
            *[dma((2,)) for _ in range(8)],
            *[dma((8,)) for _ in range(4)],
        ],
        compiler_params=pltpu.CompilerParams(
            collective_id=0, has_side_effects=True, vmem_limit_bytes=36 * 1024 * 1024
        ),
    )(images, weights)


def grad_call(*factors):
    n_pos = PR * PC
    vmem = pl.BlockSpec(memory_space=pltpu.VMEM)
    return pl.pallas_call(
        grad_kernel,
        name="rica_grad",
        out_shape=jax.ShapeDtypeStruct((n_pos, K, F), F32),
        in_specs=[vmem] * 5,
        out_specs=pl.BlockSpec(memory_space=pltpu.HBM),
        scratch_shapes=[
            pltpu.VMEM((n_pos, K, F), F32),
            pltpu.SemaphoreType.DMA((n_pos, 2)),
        ],
        compiler_params=pltpu.CompilerParams(vmem_limit_bytes=12 * 1024 * 1024),
    )(*factors)


def body(images, weights):
    images = images.reshape(CH, HEIGHT, WIDTH).transpose(0, 2, 1)
    weights = weights.reshape(PR * PC, F, K).transpose(0, 2, 1)
    images = pltpu.with_memory_space_constraint(images, pltpu.HBM)
    weights = pltpu.with_memory_space_constraint(weights, pltpu.HBM)
    factors = main_call(images, weights)
    factors = [pltpu.with_memory_space_constraint(x, pltpu.VMEM) for x in factors]
    grad = grad_call(*factors)
    return grad.transpose(0, 2, 1).reshape(PR, PC, F, K)


def solution(mesh):
    return jax.shard_map(
        body,
        mesh=mesh,
        in_specs=(P(("row", "col"), None, None, None), P("row", "col", None, None)),
        out_specs=P("row", "col", None, None),
        check_vma=False,
    )
```

```python
import jax
import jax.numpy as jnp
from jax import lax
from jax.experimental import pallas as pl
from jax.experimental.pallas import tpu as pltpu
from jax.sharding import PartitionSpec as P

MESH = pl.DeviceIdType.MESH
F32 = jnp.float32
BF16 = jnp.bfloat16

ROWS, COLS = 8, 16
DEVS = ROWS * COLS
CH, S, FIELD, PAD = 3, 4, 20, 8
K = 1200
F = 128
B = 128
HEIGHT, WIDTH = 128, 192
PR, PC = 4, 3
SPARSITY = 0.5
EPS = 1e-05

SIDES = (0, 1)
DIRS = [(dr, dc) for dr in (-1, 0, 1) for dc in (-1, 0, 1) if (dr, dc) != (0, 0)]
OUTER_Y, OUTER_X = {-1: 0, 0: 8, 1: 24}, {-1: 8, 1: 28}
INNER_Y, INNER_X = {-1: 8, 0: 8, 1: 16}, {-1: 16, 1: 20}
RIM = [CH * (288 // CH if dc == 0 else 8 * (16 if dr == 0 else 8)) for dr, dc in DIRS]


def low_rows():
    return lax.broadcasted_iota(jnp.int32, (8, 128), 0) < 4


def patch(src, p, x0, channels=range(CH)):
    low = low_rows()
    blocks = []
    for c in channels:
        for u in range(0, FIELD, 2):
            y = S * p + u
            blocks += [
                src[c, y, pl.ds(x0, 8), :],
                src[c, y, pl.ds(x0 + 8, 8), :],
                jnp.where(low, src[c, y, pl.ds(x0 + 16, 8), :], src[c, y + 1, pl.ds(x0 - 4, 8), :]),
                src[c, y + 1, pl.ds(x0 + 4, 8), :],
                src[c, y + 1, pl.ds(x0 + 12, 8), :],
            ]
    return jnp.concatenate(blocks, axis=0).astype(BF16)


def main_kernel(img_hbm, w_hbm, pat, rpat, back_out, hid_out, *scr):
    (wv, rext, hs, img, wt, strip, sb, rb, ext, cext, hext, iext, flat, edge_s, edge_r, spr_s, spr_r) = scr[:17]
    terms_s, terms_r, resid_s, resid_r = scr[17:25], scr[25:33], scr[33:41], scr[41:49]
    im_sem, w_sem, a2a_send, a2a_recv = scr[49:53]
    sems = scr[53:]
    row = lax.axis_index("row")
    col = lax.axis_index("col")
    me = row * COLS + col

    im_copy = pltpu.make_async_copy(img_hbm, img, im_sem)
    im_copy.start()

    def there(axis, side):
        at, n = (row, ROWS) if axis == "row" else (col, COLS)
        return at < n - 1 if side else at > 0

    barrier = pltpu.get_barrier_semaphore()

    def greet(i, carry):
        tr = (row + i) & (ROWS - 1)
        for j in range(COLS):
            pl.semaphore_signal(
                barrier, inc=1, device_id=(tr, (col + j) & (COLS - 1)), device_id_type=MESH
            )
        return carry

    lax.fori_loop(1, ROWS, greet, 0)
    for j in range(1, COLS):
        pl.semaphore_signal(
            barrier, inc=1, device_id=(row, (col + j) & (COLS - 1)), device_id_type=MESH
        )

    w_copy = pltpu.make_async_copy(w_hbm, wt, w_sem)
    w_copy.start()

    im_copy.wait()
    pixels = img[...].reshape(CH * WIDTH, HEIGHT).astype(F32)
    count = CH * HEIGHT * WIDTH
    center = jnp.sum(pixels, axis=(0, 1), keepdims=True) / count
    shifted = pixels - center
    variance = jnp.sum(shifted * shifted, axis=(0, 1), keepdims=True) / count
    normed = (shifted / jnp.sqrt(variance + EPS)).astype(BF16)

    planes = jnp.concatenate([normed[c * WIDTH : (c + 1) * WIDTH] for c in range(CH)], axis=1)
    yy = lax.broadcasted_iota(jnp.int32, (HEIGHT, 128), 0)
    lane = lax.broadcasted_iota(jnp.int32, (HEIGHT, 128), 1)
    where_from = []
    for c in range(CH):
        offset = jnp.where((lane >> 5) == c, yy - 4 * (lane & 31), -1)
        where_from.append(
            jnp.concatenate([jnp.where(offset == j, 1.0, 0.0) for j in range(4)], axis=1)
        )
    spread_y = jnp.concatenate(where_from, axis=0).astype(BF16)
    strips = jnp.dot(planes, spread_y, preferred_element_type=F32)
    for j in range(4):
        strip[j, 0:8, :] = jnp.zeros((8, 128), F32)
        strip[j, 8 : 8 + WIDTH, :] = strips[:, j * 128 : j * 128 + 128]
        strip[j, 8 + WIDTH : 32 + WIDTH, :] = jnp.zeros((24, 128), F32)

    def cut(t, carry):
        parts = [strip[j, pl.ds(12 * t, 32), :] for j in range(4)]
        block = jnp.concatenate(parts, axis=0).astype(BF16).T
        view = sb.at[t].reshape(CH * 64, 128)
        for c in range(CH):
            view[c * 64 : c * 64 + 16, :] = jnp.zeros((16, 128), BF16)
            view[c * 64 + 16 : c * 64 + 48, :] = block[c * 32 : c * 32 + 32]
            view[c * 64 + 48 : c * 64 + 64, :] = jnp.zeros((16, 128), BF16)
        return carry

    lax.fori_loop(0, COLS, cut, 0)

    pl.semaphore_wait(barrier, DEVS - 1)

    def send_block(c, tr, tc):
        pltpu.make_async_remote_copy(
            src_ref=sb.at[tc, c, pl.ds(7 + 2 * tr, 4)],
            dst_ref=rb.at[c, :, me],
            send_sem=a2a_send,
            recv_sem=a2a_recv.at[c],
            device_id=(tr, tc),
            device_id_type=MESH,
        ).start()

    for c in range(CH):
        pltpu.make_async_copy(
            sb.at[col, c, pl.ds(7 + 2 * row, 4)], rb.at[c, :, me], a2a_recv.at[c]
        ).start()

        def send_row(i, carry, c=c):
            tr = (row + i) & (ROWS - 1)
            for j in range(COLS):
                send_block(c, tr, (col + j) & (COLS - 1))
            return carry

        lax.fori_loop(1, ROWS, send_row, 0)
        for j in range(1, COLS):
            send_block(c, row, (col + j) & (COLS - 1))

    for side in SIDES:

        @pl.when(jnp.logical_not(there("col", side)))
        def _(side=side):
            for p in range(PR):
                hext[p, 4 * side] = jnp.zeros((F, B), BF16)
                iext[p, 4 * side] = jnp.zeros((F, B), BF16)

        @pl.when(jnp.logical_not(there("row", side)))
        def _(side=side):
            for ref in (edge_r, spr_r):
                ref[side] = jnp.zeros(ref.shape[1:], BF16)

    def near(k):
        dr, dc = DIRS[k]
        ok = None
        for axis, d in (("row", dr), ("col", dc)):
            if d:
                one = there(axis, (d + 1) // 2)
                ok = one if ok is None else ok & one
        return ok

    for k in range(8):

        @pl.when(jnp.logical_not(near(k)))
        def _(k=k):
            for ref in (terms_r[k], resid_r[k]):
                ref[...] = jnp.zeros(ref.shape, BF16)

    cext[...] = jnp.zeros(cext.shape, F32)
    w_copy.wait()

    def flip(pos, carry):
        for kb in range(0, K, 128):
            n = min(128, K - kb)
            wv[pos, :, kb : kb + n] = wt[pos, kb : kb + n, :].T
        return carry

    lax.fori_loop(0, PR * PC, flip, 0)

    mr = lax.broadcasted_iota(jnp.int32, (256, 256), 0)
    mc = lax.broadcasted_iota(jnp.int32, (256, 256), 1)
    split = jnp.where(
        mr == jnp.where(mc < 128, 2 * mc, 2 * mc - 255), 1.0, 0.0
    ).astype(BF16)

    low = low_rows()

    def unpatch(dst, terms, p, x0):
        blocks = [terms[8 * m : 8 * m + 8] for m in range(K // 8)]
        for c in range(CH):
            for u in range(0, FIELD, 2):
                y = S * p + u
                b0, b1, b2, b3, b4 = blocks[(c * FIELD + u) // 2 * 5 :][:5]
                dst[c, y, pl.ds(x0, 8), :] += b0
                dst[c, y, pl.ds(x0 + 8, 8), :] += b1
                dst[c, y, pl.ds(x0 + 16, 8), :] += jnp.where(low, b2, 0.0)
                dst[c, y + 1, pl.ds(x0 - 4, 8), :] += jnp.where(low, 0.0, b2)
                dst[c, y + 1, pl.ds(x0 + 4, 8), :] += b3
                dst[c, y + 1, pl.ds(x0 + 12, 8), :] += b4

    for c in range(CH):
        pltpu.make_async_copy(rb.at[c], rb.at[c], a2a_recv.at[c]).wait()
        for i in range(4):
            pair = rb.at[c, i].reshape(256, 128)[...]
            turned = lax.dot_general(
                pair, split, (((0,), (0,)), ((), ())), preferred_element_type=F32
            )
            for par in range(2):
                y0 = 8 * i + 4 * par
                part = turned[:, par * 128 : par * 128 + 128].reshape(4, 32, 128)
                ext[c, y0 : y0 + 4, 8:40, :] = part
        lo = 384 * c
        hi = 384 * (c + 1) if c < CH - 1 else K

        def encode(p, carry, c=c, lo=lo, hi=hi):
            zero = lax.shift_right_logical(p, 4)
            for q in range(PC):
                pos = PC * p + q
                columns = patch(ext, p, zero + (8 + S * q), [c])
                pat[pos, 400 * c : 400 * c + 400, :] = columns
                if lo < 400 * c:
                    columns = jnp.concatenate([pat[pos, lo : 400 * c, :], columns], axis=0)
                sums = jnp.dot(wv[pos, :, lo:hi], columns[: hi - lo], preferred_element_type=F32)
                if c > 0:
                    sums = sums + hs[pos]
                if c < CH - 1:
                    hs[pos] = sums
                else:
                    hidden = sums.astype(BF16)
                    hext[p, q + 1] = hidden
                    hid_out[pos] = hidden
            return carry

        lax.fori_loop(0, PR, encode, 0)

    class Exchange:
        def __init__(self, n, axis, src, dst):
            self.axis, self.src, self.dst = axis, src, dst
            self.send, self.recv = sems[2 * n], sems[2 * n + 1]

        def copy(self, side):
            step = 1 if side else -1
            to = (row + step, col) if self.axis == "row" else (row, col + step)
            return pltpu.make_async_remote_copy(
                src_ref=self.src(side),
                dst_ref=self.dst(1 - side),
                send_sem=self.send.at[side],
                recv_sem=self.recv.at[side],
                device_id=to,
                device_id_type=MESH,
            )

        def each(self, act):
            for side in SIDES:

                @pl.when(there(self.axis, side))
                def _(side=side):
                    act(side)

        def start(self):
            self.each(lambda side: self.copy(side).start())

        def arrive(self):
            self.each(lambda side: self.copy(1 - side).wait_recv())

        def sent(self):
            self.each(lambda side: self.copy(side).wait_send())

    def side_columns(ref):
        return (
            lambda side: ref.at[:, 3 if side else 1],
            lambda side: ref.at[:, 4 if side else 0],
        )

    def whole(send, recv):
        return lambda side: send.at[side], lambda side: recv.at[side]

    hidden_x = Exchange(0, "col", *side_columns(hext))
    square_x = Exchange(1, "row", *whole(edge_s, edge_r))
    inverse_x = Exchange(2, "col", *side_columns(iext))
    spread_x = Exchange(3, "row", *whole(spr_s, spr_r))

    class Around:
        def __init__(self, n, send, recv):
            self.bufs, self.sems = (send, recv), (sems[n], sems[n + 1])

        def copy(self, k):
            dr, dc = DIRS[k]
            return pltpu.make_async_remote_copy(
                src_ref=self.bufs[0][k],
                dst_ref=self.bufs[1][7 - k],
                send_sem=self.sems[0].at[k],
                recv_sem=self.sems[1].at[7 - k],
                device_id=(row + dr, col + dc),
                device_id_type=MESH,
            )

        def each(self, act):
            for k in range(8):

                @pl.when(near(k))
                def _(k=k):
                    act(k)

        def start(self):
            self.each(lambda k: self.copy(k).start())

        def arrive(self):
            self.each(lambda k: self.copy(7 - k).wait_recv())

        def sent(self):
            self.each(lambda k: self.copy(k).wait_send())

    terms_x = Around(8, terms_s, terms_r)
    resid_x = Around(10, resid_s, resid_r)

    hidden_x.start()

    def decode(p, carry):
        zero = lax.shift_right_logical(p, 4)
        for q in range(PC):
            pos = PC * p + q
            terms = jnp.dot(wt[pos], hid_out[pos], preferred_element_type=F32)
            unpatch(cext, terms, p, zero + (8 + S * q))
        return carry

    lax.fori_loop(0, PR, decode, 0)

    zero = lax.shift_right_logical(row, 8)

    def pack_rows(src, y0):
        blocks = []
        for c in range(CH):
            for y in range(y0, y0 + 8, 2):
                blocks += [
                    src[c, y, pl.ds(zero + 16, 8), :],
                    jnp.where(low, src[c, y, pl.ds(zero + 24, 8), :], src[c, y + 1, pl.ds(zero + 12, 8), :]),
                    src[c, y + 1, pl.ds(zero + 20, 8), :],
                ]
        return jnp.concatenate(blocks, axis=0).astype(BF16)

    def unpack_rows(got, y0):
        for c in range(CH):
            for n in range(4):
                at = (c * 4 + n) * 24
                yield c, y0 + 2 * n, [got[at + 8 * m : at + 8 * m + 8] for m in range(3)]

    def pack(src, k, ys, xs):
        dr, dc = DIRS[k]
        if dc == 0:
            return pack_rows(src, ys[dr])
        ny = 16 if dr == 0 else 8
        part = src[:, ys[dr] : ys[dr] + ny, pl.ds(zero + xs[dc], 8), :]
        return part.reshape(RIM[k], 128).astype(BF16)

    for k in range(8):
        terms_s[k][...] = pack(cext, k, OUTER_Y, OUTER_X)
    terms_x.start()

    hidden_x.arrive()

    def across(get):
        cells = [get(b) for b in range(PC + 2)]
        return [cells[b] + cells[b + 1] + cells[b + 2] for b in range(PC)]

    def chunk(n):
        return pl.ds(pl.multiple_of(n * 16, 16), 16)

    def squares(n, carry):
        rows16 = chunk(n)
        for p in range(PR):

            def square(b):
                v = hext[p, b, rows16, :].astype(F32)
                return v * v

            for q, total in enumerate(across(square)):
                flat[p, q, rows16, :] = total
                if p == 0:
                    edge_s[0, q, rows16, :] = total.astype(BF16)
                if p == PR - 1:
                    edge_s[1, q, rows16, :] = total.astype(BF16)
        return carry

    lax.fori_loop(0, F // 16, squares, 0)
    square_x.start()

    square_x.arrive()

    def down(q, rows16, outside):
        cells = [outside[0, q, rows16, :].astype(F32)]
        cells += [flat[p, q, rows16, :] for p in range(PR)]
        cells += [outside[1, q, rows16, :].astype(F32)]
        return [cells[p] + cells[p + 1] + cells[p + 2] for p in range(PR)]

    def pool(n, carry):
        rows16 = chunk(n)
        for q in range(PC):
            for p, total in enumerate(down(q, rows16, edge_r)):
                energy = jnp.sqrt(1.0 + total)
                iext[p, q + 1, rows16, :] = (1.0 / energy).astype(BF16)
        return carry

    lax.fori_loop(0, F // 16, pool, 0)
    inverse_x.start()

    terms_x.arrive()
    for k, (dr, dc) in enumerate(DIRS):
        got = terms_r[k][...].astype(F32)
        if dc == 0:
            for c, y, (b0, b1, b2) in unpack_rows(got, INNER_Y[dr]):
                cext[c, y, pl.ds(zero + 16, 8), :] += b0
                cext[c, y, pl.ds(zero + 24, 8), :] += jnp.where(low, b1, 0.0)
                cext[c, y + 1, pl.ds(zero + 12, 8), :] += jnp.where(low, 0.0, b1)
                cext[c, y + 1, pl.ds(zero + 20, 8), :] += b2
        else:
            ny = 16 if dr == 0 else 8
            y0 = INNER_Y[dr]
            cext[:, y0 : y0 + ny, pl.ds(zero + INNER_X[dc], 8), :] += got.reshape(CH, ny, 8, 128)
    for x, n in ((16, 8), (24, 4)):
        at = slice(x, x + n)
        resid = cext[:, 8:24, at, :] - ext[:, 8:24, at, :]
        rext[:, 8:24, at, :] = resid.astype(BF16).astype(F32)
    for k in range(8):
        resid_s[k][...] = pack(rext, k, INNER_Y, INNER_X)
    resid_x.start()

    inverse_x.arrive()

    def inverses(n, carry):
        rows16 = chunk(n)
        for p in range(PR):
            for q, total in enumerate(across(lambda b: iext[p, b, rows16, :].astype(F32))):
                flat[p, q, rows16, :] = total
                if p == 0:
                    spr_s[0, q, rows16, :] = total.astype(BF16)
                if p == PR - 1:
                    spr_s[1, q, rows16, :] = total.astype(BF16)
        return carry

    lax.fori_loop(0, F // 16, inverses, 0)
    spread_x.start()

    resid_x.arrive()
    for k in sorted(range(8), key=lambda k: DIRS[k][1] != 0):
        dr, dc = DIRS[k]
        got = resid_r[k][...].astype(F32)
        if dc == 0:
            for c, y, (b0, b1, b2) in unpack_rows(got, OUTER_Y[dr]):
                rext[c, y, pl.ds(zero + 16, 8), :] = b0
                rext[c, y, pl.ds(zero + 24, 8), :] = b1
                rext[c, y + 1, pl.ds(zero + 12, 8), :] = b1
                rext[c, y + 1, pl.ds(zero + 20, 8), :] = b2
        else:
            ny = 16 if dr == 0 else 8
            y0 = OUTER_Y[dr]
            rext[:, y0 : y0 + ny, pl.ds(zero + OUTER_X[dc], 8), :] = got.reshape(CH, ny, 8, 128)

    def backward(p, carry):
        zero = lax.shift_right_logical(p, 4)
        for q in range(PC):
            pos = PC * p + q
            columns = patch(rext, p, zero + (8 + S * q))
            rpat[pos] = columns
            hs[pos] = jnp.dot(wv[pos], columns, preferred_element_type=F32)
        return carry

    lax.fori_loop(0, PR, backward, 0)

    spread_x.arrive()

    def widen(n, carry):
        rows16 = chunk(n)
        for q in range(PC):
            for p, total in enumerate(down(q, rows16, spr_r)):
                hidden = hid_out[p * PC + q, rows16, :].astype(F32)
                back = SPARSITY * hidden * total + hs[p * PC + q, rows16, :]
                back_out[p * PC + q, rows16, :] = back.astype(BF16)
        return carry

    lax.fori_loop(0, F // 16, widen, 0)

    pltpu.make_async_copy(
        rb.at[:, :, pl.ds(0, DEVS - 1)], rb.at[:, :, pl.ds(0, DEVS - 1)], a2a_send
    ).wait()
    for exchange in (hidden_x, square_x, inverse_x, spread_x, terms_x, resid_x):
        exchange.sent()


def grad_kernel(pat, rpat, back, hid, out, stage, sems):
    halves = (slice(0, K // 2), slice(K // 2, K))
    copies = []
    for pos in range(PR * PC):
        right = jnp.concatenate([back[pos], hid[pos]], axis=1)
        for n, rows in enumerate(halves):
            left = jnp.concatenate([pat[pos, rows, :], rpat[pos, rows, :]], axis=1)
            grad = lax.dot_general(left, right, (((1,), (1,)), ((), ())), preferred_element_type=F32)
            stage[pos, rows, :] = grad * (1.0 / B)
            copy = pltpu.make_async_copy(stage.at[pos, rows], out.at[pos, rows], sems.at[pos, n])
            copy.start()
            copies.append(copy)
    for copy in copies:
        copy.wait()


def main_call(images, weights):
    dma = pltpu.SemaphoreType.DMA
    vmem = pl.BlockSpec(memory_space=pltpu.VMEM)
    hbm = pl.BlockSpec(memory_space=pltpu.HBM)
    n_pos = PR * PC
    return pl.pallas_call(
        main_kernel,
        name="rica_main",
        out_shape=(
            pltpu.VMEM((n_pos, K, B), BF16),
            pltpu.VMEM((n_pos, K, B), BF16),
            pltpu.VMEM((n_pos, F, B), BF16),
            pltpu.VMEM((n_pos, F, B), BF16),
        ),
        in_specs=[hbm, hbm],
        out_specs=(vmem,) * 4,
        scratch_shapes=[
            pltpu.VMEM((n_pos, F, K), BF16),
            pltpu.VMEM((CH, 32, 40, 128), F32),
            pltpu.VMEM((n_pos, F, B), F32),
            pltpu.VMEM((CH, WIDTH, HEIGHT), BF16),
            pltpu.VMEM((n_pos, K, F), BF16),
            pltpu.VMEM((4, WIDTH + 32, 128), F32),
            pltpu.VMEM((COLS, CH, 32, 2, 128), BF16),
            pltpu.VMEM((CH, 4, DEVS, 2, 128), BF16),
            pltpu.VMEM((CH, 32, 40, 128), F32),
            pltpu.VMEM((CH, 32, 40, 128), F32),
            pltpu.VMEM((PR, PC + 2, F, B), BF16),
            pltpu.VMEM((PR, PC + 2, F, B), BF16),
            pltpu.VMEM((PR, PC, F, B), F32),
            *[pltpu.VMEM((2, PC, F, B), BF16) for _ in range(4)],
            *[pltpu.VMEM((n, 128), BF16) for _ in range(4) for n in RIM],
            *[dma for _ in range(3)],
            dma((CH,)),
            *[dma((2,)) for _ in range(8)],
            *[dma((8,)) for _ in range(4)],
        ],
        compiler_params=pltpu.CompilerParams(
            collective_id=0, has_side_effects=True, vmem_limit_bytes=36 * 1024 * 1024
        ),
    )(images, weights)


def grad_call(*factors):
    n_pos = PR * PC
    vmem = pl.BlockSpec(memory_space=pltpu.VMEM)
    return pl.pallas_call(
        grad_kernel,
        name="rica_grad",
        out_shape=jax.ShapeDtypeStruct((n_pos, K, F), F32),
        in_specs=[vmem] * 4,
        out_specs=pl.BlockSpec(memory_space=pltpu.HBM),
        scratch_shapes=[
            pltpu.VMEM((n_pos, K, F), F32),
            pltpu.SemaphoreType.DMA((n_pos, 2)),
        ],
        compiler_params=pltpu.CompilerParams(vmem_limit_bytes=12 * 1024 * 1024),
    )(*factors)


def body(images, weights):
    images = images.reshape(CH, HEIGHT, WIDTH).transpose(0, 2, 1)
    weights = weights.reshape(PR * PC, F, K).transpose(0, 2, 1)
    images = pltpu.with_memory_space_constraint(images, pltpu.HBM)
    weights = pltpu.with_memory_space_constraint(weights, pltpu.HBM)
    factors = main_call(images, weights)
    factors = [pltpu.with_memory_space_constraint(x, pltpu.VMEM) for x in factors]
    grad = grad_call(*factors)
    return grad.transpose(0, 2, 1).reshape(PR, PC, F, K)


def solution(mesh):
    return jax.shard_map(
        body,
        mesh=mesh,
        in_specs=(P(("row", "col"), None, None, None), P("row", "col", None, None)),
        out_specs=P("row", "col", None, None),
        check_vma=False,
    )
```

```python
import jax
import jax.numpy as jnp
from jax import lax
from jax.experimental import pallas as pl
from jax.experimental.pallas import tpu as pltpu
from jax.sharding import PartitionSpec as P

MESH = pl.DeviceIdType.MESH
F32 = jnp.float32
BF16 = jnp.bfloat16

ROWS, COLS = 8, 16
DEVS = ROWS * COLS
CH, S, FIELD, PAD = 3, 4, 20, 8
K = 1200
F = 128
B = 128
HEIGHT, WIDTH = 128, 192
PR, PC = 4, 3
SPARSITY = 0.5
EPS = 1e-05

SIDES = (0, 1)
DIRS = [(dr, dc) for dr in (-1, 0, 1) for dc in (-1, 0, 1) if (dr, dc) != (0, 0)]
OUTER_Y, OUTER_X = {-1: 0, 0: 8, 1: 24}, {-1: 8, 1: 28}
INNER_Y, INNER_X = {-1: 8, 0: 8, 1: 16}, {-1: 16, 1: 20}
RIM = [CH * (288 // CH if dc == 0 else 8 * (16 if dr == 0 else 8)) for dr, dc in DIRS]


def low_rows():
    return lax.broadcasted_iota(jnp.int32, (8, 128), 0) < 4


def patch(src, p, x0, channels=range(CH)):
    low = low_rows()
    blocks = []
    for c in channels:
        for u in range(0, FIELD, 2):
            y = S * p + u
            blocks += [
                src[c, y, pl.ds(x0, 8), :],
                src[c, y, pl.ds(x0 + 8, 8), :],
                jnp.where(low, src[c, y, pl.ds(x0 + 16, 8), :], src[c, y + 1, pl.ds(x0 - 4, 8), :]),
                src[c, y + 1, pl.ds(x0 + 4, 8), :],
                src[c, y + 1, pl.ds(x0 + 12, 8), :],
            ]
    return jnp.concatenate(blocks, axis=0).astype(BF16)


def main_kernel(img_hbm, w_hbm, pat, rpat, back_out, hid_out, *scr):
    (wv, rext, hs, img, wt, strip, sb, rb, ext, cext, hext, iext, flat, edge_s, edge_r, spr_s, spr_r) = scr[:17]
    terms_s, terms_r, resid_s, resid_r = scr[17:25], scr[25:33], scr[33:41], scr[41:49]
    terms_t, resid_t = scr[49:51], scr[51:53]
    im_sem, w_sem, a2a_send, a2a_recv = scr[53:57]
    sems = scr[57:]
    row = lax.axis_index("row")
    col = lax.axis_index("col")
    me = row * COLS + col

    im_copy = pltpu.make_async_copy(img_hbm, img, im_sem)
    im_copy.start()

    def there(axis, side):
        at, n = (row, ROWS) if axis == "row" else (col, COLS)
        return at < n - 1 if side else at > 0

    barrier = pltpu.get_barrier_semaphore()

    def greet(i, carry):
        tr = (row + i) & (ROWS - 1)
        for j in range(COLS):
            pl.semaphore_signal(
                barrier, inc=1, device_id=(tr, (col + j) & (COLS - 1)), device_id_type=MESH
            )
        return carry

    lax.fori_loop(1, ROWS, greet, 0)
    for j in range(1, COLS):
        pl.semaphore_signal(
            barrier, inc=1, device_id=(row, (col + j) & (COLS - 1)), device_id_type=MESH
        )

    w_copy = pltpu.make_async_copy(w_hbm, wt, w_sem)
    w_copy.start()

    im_copy.wait()
    pixels = img[...].reshape(CH * WIDTH, HEIGHT).astype(F32)
    count = CH * HEIGHT * WIDTH
    center = jnp.sum(pixels, axis=(0, 1), keepdims=True) / count
    shifted = pixels - center
    variance = jnp.sum(shifted * shifted, axis=(0, 1), keepdims=True) / count
    normed = (shifted / jnp.sqrt(variance + EPS)).astype(BF16)

    planes = jnp.concatenate([normed[c * WIDTH : (c + 1) * WIDTH] for c in range(CH)], axis=1)
    yy = lax.broadcasted_iota(jnp.int32, (HEIGHT, 128), 0)
    lane = lax.broadcasted_iota(jnp.int32, (HEIGHT, 128), 1)
    where_from = []
    for c in range(CH):
        offset = jnp.where((lane >> 5) == c, yy - 4 * (lane & 31), -1)
        where_from.append(
            jnp.concatenate([jnp.where(offset == j, 1.0, 0.0) for j in range(4)], axis=1)
        )
    spread_y = jnp.concatenate(where_from, axis=0).astype(BF16)
    strips = jnp.dot(planes, spread_y, preferred_element_type=F32)
    for j in range(4):
        strip[j, 0:8, :] = jnp.zeros((8, 128), F32)
        strip[j, 8 : 8 + WIDTH, :] = strips[:, j * 128 : j * 128 + 128]
        strip[j, 8 + WIDTH : 32 + WIDTH, :] = jnp.zeros((24, 128), F32)

    def cut(t, carry):
        parts = [strip[j, pl.ds(12 * t, 32), :] for j in range(4)]
        block = jnp.concatenate(parts, axis=0).astype(BF16).T
        view = sb.at[t].reshape(CH * 64, 128)
        for c in range(CH):
            view[c * 64 : c * 64 + 16, :] = jnp.zeros((16, 128), BF16)
            view[c * 64 + 16 : c * 64 + 48, :] = block[c * 32 : c * 32 + 32]
            view[c * 64 + 48 : c * 64 + 64, :] = jnp.zeros((16, 128), BF16)
        return carry

    lax.fori_loop(0, COLS, cut, 0)

    pl.semaphore_wait(barrier, DEVS - 1)

    def send_block(c, tr, tc):
        pltpu.make_async_remote_copy(
            src_ref=sb.at[tc, c, pl.ds(7 + 2 * tr, 4)],
            dst_ref=rb.at[c, :, me],
            send_sem=a2a_send,
            recv_sem=a2a_recv.at[c],
            device_id=(tr, tc),
            device_id_type=MESH,
        ).start()

    for c in range(CH):
        pltpu.make_async_copy(
            sb.at[col, c, pl.ds(7 + 2 * row, 4)], rb.at[c, :, me], a2a_recv.at[c]
        ).start()

        def send_row(i, carry, c=c):
            tr = (row + i) & (ROWS - 1)
            for j in range(COLS):
                send_block(c, tr, (col + j) & (COLS - 1))
            return carry

        lax.fori_loop(1, ROWS, send_row, 0)
        for j in range(1, COLS):
            send_block(c, row, (col + j) & (COLS - 1))

    for side in SIDES:

        @pl.when(jnp.logical_not(there("col", side)))
        def _(side=side):
            for p in range(PR):
                hext[p, 4 * side] = jnp.zeros((F, B), BF16)
                iext[p, 4 * side] = jnp.zeros((F, B), BF16)

        @pl.when(jnp.logical_not(there("row", side)))
        def _(side=side):
            for ref in (edge_r, spr_r):
                ref[side] = jnp.zeros(ref.shape[1:], BF16)

    def near(k):
        dr, dc = DIRS[k]
        ok = None
        for axis, d in (("row", dr), ("col", dc)):
            if d:
                one = there(axis, (d + 1) // 2)
                ok = one if ok is None else ok & one
        return ok

    for k in range(8):

        @pl.when(jnp.logical_not(near(k)))
        def _(k=k):
            for ref in (terms_r[k], resid_r[k]):
                ref[...] = jnp.zeros(ref.shape, BF16)

    cext[...] = jnp.zeros(cext.shape, F32)
    w_copy.wait()

    def flip(pos, carry):
        for kb in range(0, K, 128):
            n = min(128, K - kb)
            wv[pos, :, kb : kb + n] = wt[pos, kb : kb + n, :].T
        return carry

    lax.fori_loop(0, PR * PC, flip, 0)

    mr = lax.broadcasted_iota(jnp.int32, (256, 256), 0)
    mc = lax.broadcasted_iota(jnp.int32, (256, 256), 1)
    split = jnp.where(
        mr == jnp.where(mc < 128, 2 * mc, 2 * mc - 255), 1.0, 0.0
    ).astype(BF16)

    low = low_rows()

    def unpatch(dst, terms, p, x0):
        blocks = [terms[8 * m : 8 * m + 8] for m in range(K // 8)]
        for c in range(CH):
            for u in range(0, FIELD, 2):
                y = S * p + u
                b0, b1, b2, b3, b4 = blocks[(c * FIELD + u) // 2 * 5 :][:5]
                dst[c, y, pl.ds(x0, 8), :] += b0
                dst[c, y, pl.ds(x0 + 8, 8), :] += b1
                dst[c, y, pl.ds(x0 + 16, 8), :] += jnp.where(low, b2, 0.0)
                dst[c, y + 1, pl.ds(x0 - 4, 8), :] += jnp.where(low, 0.0, b2)
                dst[c, y + 1, pl.ds(x0 + 4, 8), :] += b3
                dst[c, y + 1, pl.ds(x0 + 12, 8), :] += b4

    for c in range(CH):
        pltpu.make_async_copy(rb.at[c], rb.at[c], a2a_recv.at[c]).wait()
        for i in range(4):
            pair = rb.at[c, i].reshape(256, 128)[...]
            turned = lax.dot_general(
                pair, split, (((0,), (0,)), ((), ())), preferred_element_type=F32
            )
            for par in range(2):
                y0 = 8 * i + 4 * par
                part = turned[:, par * 128 : par * 128 + 128].reshape(4, 32, 128)
                ext[c, y0 : y0 + 4, 8:40, :] = part
        lo = 384 * c
        hi = 384 * (c + 1) if c < CH - 1 else K

        def encode(p, carry, c=c, lo=lo, hi=hi):
            zero = lax.shift_right_logical(p, 4)
            for q in range(PC):
                pos = PC * p + q
                columns = patch(ext, p, zero + (8 + S * q), [c])
                pat[pos, 400 * c : 400 * c + 400, :] = columns
                if lo < 400 * c:
                    columns = jnp.concatenate([pat[pos, lo : 400 * c, :], columns], axis=0)
                sums = jnp.dot(wv[pos, :, lo:hi], columns[: hi - lo], preferred_element_type=F32)
                if c > 0:
                    sums = sums + hs[pos]
                if c < CH - 1:
                    hs[pos] = sums
                else:
                    hidden = sums.astype(BF16)
                    hext[p, q + 1] = hidden
                    hid_out[pos] = hidden
            return carry

        lax.fori_loop(0, PR, encode, 0)

    class Exchange:
        def __init__(self, n, axis, src, dst):
            self.axis, self.src, self.dst = axis, src, dst
            self.send, self.recv = sems[2 * n], sems[2 * n + 1]

        def copy(self, side):
            step = 1 if side else -1
            to = (row + step, col) if self.axis == "row" else (row, col + step)
            return pltpu.make_async_remote_copy(
                src_ref=self.src(side),
                dst_ref=self.dst(1 - side),
                send_sem=self.send.at[side],
                recv_sem=self.recv.at[side],
                device_id=to,
                device_id_type=MESH,
            )

        def each(self, act):
            for side in SIDES:

                @pl.when(there(self.axis, side))
                def _(side=side):
                    act(side)

        def start(self):
            self.each(lambda side: self.copy(side).start())

        def arrive(self):
            self.each(lambda side: self.copy(1 - side).wait_recv())

        def sent(self):
            self.each(lambda side: self.copy(side).wait_send())

    def side_columns(ref):
        return (
            lambda side: ref.at[:, 3 if side else 1],
            lambda side: ref.at[:, 4 if side else 0],
        )

    def whole(send, recv):
        return lambda side: send.at[side], lambda side: recv.at[side]

    hidden_x = Exchange(0, "col", *side_columns(hext))
    square_x = Exchange(1, "row", *whole(edge_s, edge_r))
    inverse_x = Exchange(2, "col", *side_columns(iext))
    spread_x = Exchange(3, "row", *whole(spr_s, spr_r))

    half = ROWS // 2

    def crosses(k):
        dr, dc = DIRS[k]
        return row == (half - 1 if dr > 0 else half) if dr and dc else None

    class Around:
        def __init__(self, n, send, recv, through):
            self.bufs, self.sems = (send, recv), sems[n : n + 4]
            self.through = through

        def copy(self, k):
            dr, dc = DIRS[k]
            return pltpu.make_async_remote_copy(
                src_ref=self.bufs[0][k],
                dst_ref=self.bufs[1][7 - k],
                send_sem=self.sems[0].at[k],
                recv_sem=self.sems[1].at[7 - k],
                device_id=(row + dr, col + dc),
                device_id_type=MESH,
            )

        def to_relay(self, k):
            dr, dc = DIRS[k]
            return pltpu.make_async_remote_copy(
                src_ref=self.bufs[0][k],
                dst_ref=self.through[(dc + 1) // 2],
                send_sem=self.sems[0].at[k],
                recv_sem=self.sems[2].at[(dc + 1) // 2],
                device_id=(row - 3 * dr, col),
                device_id_type=MESH,
            )

        def from_relay(self, k):
            dr, dc = DIRS[k]
            return pltpu.make_async_remote_copy(
                src_ref=self.through[(dc + 1) // 2],
                dst_ref=self.bufs[1][7 - k],
                send_sem=self.sems[3].at[(dc + 1) // 2],
                recv_sem=self.sems[1].at[7 - k],
                device_id=(row + half * dr, col + dc),
                device_id_type=MESH,
            )

        def each(self, act):
            for k in range(8):

                @pl.when(near(k))
                def _(k=k):
                    act(k)

        def start(self):
            for k in range(8):
                apart = crosses(k)
                if apart is None:

                    @pl.when(near(k))
                    def _(k=k):
                        self.copy(k).start()

                else:

                    @pl.when(near(k) & apart)
                    def _(k=k):
                        self.to_relay(k).start()

                    @pl.when(near(k) & jnp.logical_not(apart))
                    def _(k=k):
                        self.copy(k).start()

        def relays(self, act):
            for k, (dr, dc) in enumerate(DIRS):
                if dr and dc:

                    @pl.when((row == (0 if dr > 0 else ROWS - 1)) & there("col", (dc + 1) // 2))
                    def _(k=k):
                        act(k)

        def relay(self):
            def pass_on(k):
                slot = (DIRS[k][1] + 1) // 2
                held = self.through[slot]
                pltpu.make_async_copy(held, held, self.sems[2].at[slot]).wait()
                self.from_relay(k).start()

            self.relays(pass_on)

        def arrive(self):
            self.each(lambda k: self.copy(7 - k).wait_recv())

        def sent(self):
            self.each(lambda k: self.copy(k).wait_send())
            self.relays(lambda k: self.from_relay(k).wait_send())

    terms_x = Around(8, terms_s, terms_r, terms_t)
    resid_x = Around(12, resid_s, resid_r, resid_t)

    hidden_x.start()

    def decode(p, carry):
        zero = lax.shift_right_logical(p, 4)
        for q in range(PC):
            pos = PC * p + q
            terms = jnp.dot(wt[pos], hid_out[pos], preferred_element_type=F32)
            unpatch(cext, terms, p, zero + (8 + S * q))
        return carry

    lax.fori_loop(0, PR, decode, 0)

    zero = lax.shift_right_logical(row, 8)

    def pack_rows(src, y0):
        blocks = []
        for c in range(CH):
            for y in range(y0, y0 + 8, 2):
                blocks += [
                    src[c, y, pl.ds(zero + 16, 8), :],
                    jnp.where(low, src[c, y, pl.ds(zero + 24, 8), :], src[c, y + 1, pl.ds(zero + 12, 8), :]),
                    src[c, y + 1, pl.ds(zero + 20, 8), :],
                ]
        return jnp.concatenate(blocks, axis=0).astype(BF16)

    def unpack_rows(got, y0):
        for c in range(CH):
            for n in range(4):
                at = (c * 4 + n) * 24
                yield c, y0 + 2 * n, [got[at + 8 * m : at + 8 * m + 8] for m in range(3)]

    def pack(src, k, ys, xs):
        dr, dc = DIRS[k]
        if dc == 0:
            return pack_rows(src, ys[dr])
        ny = 16 if dr == 0 else 8
        part = src[:, ys[dr] : ys[dr] + ny, pl.ds(zero + xs[dc], 8), :]
        return part.reshape(RIM[k], 128).astype(BF16)

    for k in range(8):
        terms_s[k][...] = pack(cext, k, OUTER_Y, OUTER_X)
    terms_x.start()

    hidden_x.arrive()

    def across(get):
        cells = [get(b) for b in range(PC + 2)]
        return [cells[b] + cells[b + 1] + cells[b + 2] for b in range(PC)]

    def chunk(n):
        return pl.ds(pl.multiple_of(n * 16, 16), 16)

    def squares(n, carry):
        rows16 = chunk(n)
        for p in range(PR):

            def square(b):
                v = hext[p, b, rows16, :].astype(F32)
                return v * v

            for q, total in enumerate(across(square)):
                flat[p, q, rows16, :] = total
                if p == 0:
                    edge_s[0, q, rows16, :] = total.astype(BF16)
                if p == PR - 1:
                    edge_s[1, q, rows16, :] = total.astype(BF16)
        return carry

    lax.fori_loop(0, F // 16, squares, 0)
    square_x.start()
    terms_x.relay()

    square_x.arrive()

    def down(q, rows16, outside):
        cells = [outside[0, q, rows16, :].astype(F32)]
        cells += [flat[p, q, rows16, :] for p in range(PR)]
        cells += [outside[1, q, rows16, :].astype(F32)]
        return [cells[p] + cells[p + 1] + cells[p + 2] for p in range(PR)]

    def pool(n, carry):
        rows16 = chunk(n)
        for q in range(PC):
            for p, total in enumerate(down(q, rows16, edge_r)):
                energy = jnp.sqrt(1.0 + total)
                iext[p, q + 1, rows16, :] = (1.0 / energy).astype(BF16)
        return carry

    lax.fori_loop(0, F // 16, pool, 0)
    inverse_x.start()

    terms_x.arrive()
    for k, (dr, dc) in enumerate(DIRS):
        got = terms_r[k][...].astype(F32)
        if dc == 0:
            for c, y, (b0, b1, b2) in unpack_rows(got, INNER_Y[dr]):
                cext[c, y, pl.ds(zero + 16, 8), :] += b0
                cext[c, y, pl.ds(zero + 24, 8), :] += jnp.where(low, b1, 0.0)
                cext[c, y + 1, pl.ds(zero + 12, 8), :] += jnp.where(low, 0.0, b1)
                cext[c, y + 1, pl.ds(zero + 20, 8), :] += b2
        else:
            ny = 16 if dr == 0 else 8
            y0 = INNER_Y[dr]
            cext[:, y0 : y0 + ny, pl.ds(zero + INNER_X[dc], 8), :] += got.reshape(CH, ny, 8, 128)
    for x, n in ((16, 8), (24, 4)):
        at = slice(x, x + n)
        resid = cext[:, 8:24, at, :] - ext[:, 8:24, at, :]
        rext[:, 8:24, at, :] = resid.astype(BF16).astype(F32)
    for k in range(8):
        resid_s[k][...] = pack(rext, k, INNER_Y, INNER_X)
    resid_x.start()

    inverse_x.arrive()

    def inverses(n, carry):
        rows16 = chunk(n)
        for p in range(PR):
            for q, total in enumerate(across(lambda b: iext[p, b, rows16, :].astype(F32))):
                flat[p, q, rows16, :] = total
                if p == 0:
                    spr_s[0, q, rows16, :] = total.astype(BF16)
                if p == PR - 1:
                    spr_s[1, q, rows16, :] = total.astype(BF16)
        return carry

    lax.fori_loop(0, F // 16, inverses, 0)
    spread_x.start()
    resid_x.relay()

    resid_x.arrive()
    for k in sorted(range(8), key=lambda k: DIRS[k][1] != 0):
        dr, dc = DIRS[k]
        got = resid_r[k][...].astype(F32)
        if dc == 0:
            for c, y, (b0, b1, b2) in unpack_rows(got, OUTER_Y[dr]):
                rext[c, y, pl.ds(zero + 16, 8), :] = b0
                rext[c, y, pl.ds(zero + 24, 8), :] = b1
                rext[c, y + 1, pl.ds(zero + 12, 8), :] = b1
                rext[c, y + 1, pl.ds(zero + 20, 8), :] = b2
        else:
            ny = 16 if dr == 0 else 8
            y0 = OUTER_Y[dr]
            rext[:, y0 : y0 + ny, pl.ds(zero + OUTER_X[dc], 8), :] = got.reshape(CH, ny, 8, 128)

    def backward(p, carry):
        zero = lax.shift_right_logical(p, 4)
        for q in range(PC):
            pos = PC * p + q
            columns = patch(rext, p, zero + (8 + S * q))
            rpat[pos] = columns
            hs[pos] = jnp.dot(wv[pos], columns, preferred_element_type=F32)
        return carry

    lax.fori_loop(0, PR, backward, 0)

    spread_x.arrive()

    def widen(n, carry):
        rows16 = chunk(n)
        for q in range(PC):
            for p, total in enumerate(down(q, rows16, spr_r)):
                hidden = hid_out[p * PC + q, rows16, :].astype(F32)
                back = SPARSITY * hidden * total + hs[p * PC + q, rows16, :]
                back_out[p * PC + q, rows16, :] = back.astype(BF16)
        return carry

    lax.fori_loop(0, F // 16, widen, 0)

    pltpu.make_async_copy(
        rb.at[:, :, pl.ds(0, DEVS - 1)], rb.at[:, :, pl.ds(0, DEVS - 1)], a2a_send
    ).wait()
    for exchange in (hidden_x, square_x, inverse_x, spread_x, terms_x, resid_x):
        exchange.sent()


def grad_kernel(pat, rpat, back, hid, out, stage, sems):
    halves = (slice(0, K // 2), slice(K // 2, K))
    copies = []
    for pos in range(PR * PC):
        right = jnp.concatenate([back[pos], hid[pos]], axis=1)
        for n, rows in enumerate(halves):
            left = jnp.concatenate([pat[pos, rows, :], rpat[pos, rows, :]], axis=1)
            grad = lax.dot_general(left, right, (((1,), (1,)), ((), ())), preferred_element_type=F32)
            stage[pos, rows, :] = grad * (1.0 / B)
            copy = pltpu.make_async_copy(stage.at[pos, rows], out.at[pos, rows], sems.at[pos, n])
            copy.start()
            copies.append(copy)
    for copy in copies:
        copy.wait()


def main_call(images, weights):
    dma = pltpu.SemaphoreType.DMA
    vmem = pl.BlockSpec(memory_space=pltpu.VMEM)
    hbm = pl.BlockSpec(memory_space=pltpu.HBM)
    n_pos = PR * PC
    return pl.pallas_call(
        main_kernel,
        name="rica_main",
        out_shape=(
            pltpu.VMEM((n_pos, K, B), BF16),
            pltpu.VMEM((n_pos, K, B), BF16),
            pltpu.VMEM((n_pos, F, B), BF16),
            pltpu.VMEM((n_pos, F, B), BF16),
        ),
        in_specs=[hbm, hbm],
        out_specs=(vmem,) * 4,
        scratch_shapes=[
            pltpu.VMEM((n_pos, F, K), BF16),
            pltpu.VMEM((CH, 32, 40, 128), F32),
            pltpu.VMEM((n_pos, F, B), F32),
            pltpu.VMEM((CH, WIDTH, HEIGHT), BF16),
            pltpu.VMEM((n_pos, K, F), BF16),
            pltpu.VMEM((4, WIDTH + 32, 128), F32),
            pltpu.VMEM((COLS, CH, 32, 2, 128), BF16),
            pltpu.VMEM((CH, 4, DEVS, 2, 128), BF16),
            pltpu.VMEM((CH, 32, 40, 128), F32),
            pltpu.VMEM((CH, 32, 40, 128), F32),
            pltpu.VMEM((PR, PC + 2, F, B), BF16),
            pltpu.VMEM((PR, PC + 2, F, B), BF16),
            pltpu.VMEM((PR, PC, F, B), F32),
            *[pltpu.VMEM((2, PC, F, B), BF16) for _ in range(4)],
            *[pltpu.VMEM((n, 128), BF16) for _ in range(4) for n in RIM],
            *[pltpu.VMEM((RIM[0], 128), BF16) for _ in range(4)],
            *[dma for _ in range(3)],
            dma((CH,)),
            *[dma((2,)) for _ in range(8)],
            *[dma((n,)) for _ in range(2) for n in (8, 8, 2, 2)],
        ],
        compiler_params=pltpu.CompilerParams(
            collective_id=0, has_side_effects=True, vmem_limit_bytes=36 * 1024 * 1024
        ),
    )(images, weights)


def grad_call(*factors):
    n_pos = PR * PC
    vmem = pl.BlockSpec(memory_space=pltpu.VMEM)
    return pl.pallas_call(
        grad_kernel,
        name="rica_grad",
        out_shape=jax.ShapeDtypeStruct((n_pos, K, F), F32),
        in_specs=[vmem] * 4,
        out_specs=pl.BlockSpec(memory_space=pltpu.HBM),
        scratch_shapes=[
            pltpu.VMEM((n_pos, K, F), F32),
            pltpu.SemaphoreType.DMA((n_pos, 2)),
        ],
        compiler_params=pltpu.CompilerParams(vmem_limit_bytes=12 * 1024 * 1024),
    )(*factors)


def body(images, weights):
    images = images.reshape(CH, HEIGHT, WIDTH).transpose(0, 2, 1)
    weights = weights.reshape(PR * PC, F, K).transpose(0, 2, 1)
    images = pltpu.with_memory_space_constraint(images, pltpu.HBM)
    weights = pltpu.with_memory_space_constraint(weights, pltpu.HBM)
    factors = main_call(images, weights)
    factors = [pltpu.with_memory_space_constraint(x, pltpu.VMEM) for x in factors]
    grad = grad_call(*factors)
    return grad.transpose(0, 2, 1).reshape(PR, PC, F, K)


def solution(mesh):
    return jax.shard_map(
        body,
        mesh=mesh,
        in_specs=(P(("row", "col"), None, None, None), P("row", "col", None, None)),
        out_specs=P("row", "col", None, None),
        check_vma=False,
    )
```

```python
import jax
import jax.numpy as jnp
from jax import lax
from jax.experimental import pallas as pl
from jax.experimental.pallas import tpu as pltpu
from jax.sharding import PartitionSpec as P

MESH = pl.DeviceIdType.MESH
F32 = jnp.float32
BF16 = jnp.bfloat16

ROWS, COLS = 8, 16
DEVS = ROWS * COLS
CH, S, FIELD, PAD = 3, 4, 20, 8
K = 1200
F = 128
B = 128
HEIGHT, WIDTH = 128, 192
PR, PC = 4, 3
SPARSITY = 0.5
EPS = 1e-05

SIDES = (0, 1)
DIRS = [(dr, dc) for dr in (-1, 0, 1) for dc in (-1, 0, 1) if (dr, dc) != (0, 0)]
OUTER_Y, OUTER_X = {-1: 0, 0: 8, 1: 24}, {-1: 8, 1: 28}
INNER_Y, INNER_X = {-1: 8, 0: 8, 1: 16}, {-1: 16, 1: 20}
RIM = [CH * (288 // CH if dc == 0 else 8 * (16 if dr == 0 else 8)) for dr, dc in DIRS]


def low_rows():
    return lax.broadcasted_iota(jnp.int32, (8, 128), 0) < 4


def patch(src, p, x0, channels=range(CH)):
    low = low_rows()
    blocks = []
    for c in channels:
        for u in range(0, FIELD, 2):
            y = S * p + u
            blocks += [
                src[c, y, pl.ds(x0, 8), :],
                src[c, y, pl.ds(x0 + 8, 8), :],
                jnp.where(low, src[c, y, pl.ds(x0 + 16, 8), :], src[c, y + 1, pl.ds(x0 - 4, 8), :]),
                src[c, y + 1, pl.ds(x0 + 4, 8), :],
                src[c, y + 1, pl.ds(x0 + 12, 8), :],
            ]
    return jnp.concatenate(blocks, axis=0).astype(BF16)


def main_kernel(img_hbm, w_hbm, pat, rpat, back_out, hid_out, *scr):
    (wv, rext, hs, img, wt, strip, sb, rb, ext, cext, hext, iext, flat, edge_s, edge_r, spr_s, spr_r) = scr[:17]
    terms_s, terms_r, resid_s, resid_r = scr[17:25], scr[25:33], scr[33:41], scr[41:49]
    terms_t, resid_t = scr[49:51], scr[51:53]
    im_sem, w_sem, a2a_send, a2a_recv = scr[53:57]
    sems = scr[57:]
    row = lax.axis_index("row")
    col = lax.axis_index("col")
    me = row * COLS + col

    im_copy = pltpu.make_async_copy(img_hbm, img, im_sem)
    im_copy.start()

    def there(axis, side):
        at, n = (row, ROWS) if axis == "row" else (col, COLS)
        return at < n - 1 if side else at > 0

    barrier = pltpu.get_barrier_semaphore()

    def greet(i, carry):
        tr = (row + i) & (ROWS - 1)
        for j in range(COLS):
            pl.semaphore_signal(
                barrier, inc=1, device_id=(tr, (col + j) & (COLS - 1)), device_id_type=MESH
            )
        return carry

    lax.fori_loop(2, ROWS, greet, 0)
    greet(1, 0)
    for j in range(1, COLS):
        pl.semaphore_signal(
            barrier, inc=1, device_id=(row, (col + j) & (COLS - 1)), device_id_type=MESH
        )

    w_copy = pltpu.make_async_copy(w_hbm, wt, w_sem)
    w_copy.start()

    im_copy.wait()
    pixels = img[...].reshape(CH * WIDTH, HEIGHT).astype(F32)
    count = CH * HEIGHT * WIDTH
    center = jnp.sum(pixels, axis=(0, 1), keepdims=True) / count
    shifted = pixels - center
    variance = jnp.sum(shifted * shifted, axis=(0, 1), keepdims=True) / count
    normed = (shifted / jnp.sqrt(variance + EPS)).astype(BF16)

    planes = jnp.concatenate([normed[c * WIDTH : (c + 1) * WIDTH] for c in range(CH)], axis=1)
    yy = lax.broadcasted_iota(jnp.int32, (HEIGHT, 128), 0)
    lane = lax.broadcasted_iota(jnp.int32, (HEIGHT, 128), 1)
    where_from = []
    for c in range(CH):
        offset = jnp.where((lane >> 5) == c, yy - 4 * (lane & 31), -1)
        where_from.append(
            jnp.concatenate([jnp.where(offset == j, 1.0, 0.0) for j in range(4)], axis=1)
        )
    spread_y = jnp.concatenate(where_from, axis=0).astype(BF16)
    strips = jnp.dot(planes, spread_y, preferred_element_type=F32)
    for j in range(4):
        strip[j, 0:8, :] = jnp.zeros((8, 128), F32)
        strip[j, 8 : 8 + WIDTH, :] = strips[:, j * 128 : j * 128 + 128]
        strip[j, 8 + WIDTH : 32 + WIDTH, :] = jnp.zeros((24, 128), F32)

    def cut(t, carry):
        parts = [strip[j, pl.ds(12 * t, 32), :] for j in range(4)]
        block = jnp.concatenate(parts, axis=0).astype(BF16).T
        view = sb.at[t].reshape(CH * 64, 128)
        for c in range(CH):
            view[c * 64 : c * 64 + 16, :] = jnp.zeros((16, 128), BF16)
            view[c * 64 + 16 : c * 64 + 48, :] = block[c * 32 : c * 32 + 32]
            view[c * 64 + 48 : c * 64 + 64, :] = jnp.zeros((16, 128), BF16)
        return carry

    lax.fori_loop(0, COLS, cut, 0)

    pl.semaphore_wait(barrier, DEVS - 1)

    def send_block(c, tr, tc):
        pltpu.make_async_remote_copy(
            src_ref=sb.at[tc, c, pl.ds(7 + 2 * tr, 4)],
            dst_ref=rb.at[c, :, me],
            send_sem=a2a_send,
            recv_sem=a2a_recv.at[c],
            device_id=(tr, tc),
            device_id_type=MESH,
        ).start()

    for c in range(CH):
        pltpu.make_async_copy(
            sb.at[col, c, pl.ds(7 + 2 * row, 4)], rb.at[c, :, me], a2a_recv.at[c]
        ).start()

        def send_row(i, carry, c=c):
            tr = (row + i) & (ROWS - 1)
            for j in range(COLS):
                send_block(c, tr, (col + j) & (COLS - 1))
            return carry

        lax.fori_loop(2, ROWS, send_row, 0)
        send_row(1, 0)
        for j in range(1, COLS):
            send_block(c, row, (col + j) & (COLS - 1))

    for side in SIDES:

        @pl.when(jnp.logical_not(there("col", side)))
        def _(side=side):
            for p in range(PR):
                hext[p, 4 * side] = jnp.zeros((F, B), BF16)
                iext[p, 4 * side] = jnp.zeros((F, B), BF16)

        @pl.when(jnp.logical_not(there("row", side)))
        def _(side=side):
            for ref in (edge_r, spr_r):
                ref[side] = jnp.zeros(ref.shape[1:], BF16)

    def near(k):
        dr, dc = DIRS[k]
        ok = None
        for axis, d in (("row", dr), ("col", dc)):
            if d:
                one = there(axis, (d + 1) // 2)
                ok = one if ok is None else ok & one
        return ok

    for k in range(8):

        @pl.when(jnp.logical_not(near(k)))
        def _(k=k):
            for ref in (terms_r[k], resid_r[k]):
                ref[...] = jnp.zeros(ref.shape, BF16)

    cext[...] = jnp.zeros(cext.shape, F32)
    w_copy.wait()

    def flip(pos, carry):
        for kb in range(0, K, 128):
            n = min(128, K - kb)
            wv[pos, :, kb : kb + n] = wt[pos, kb : kb + n, :].T
        return carry

    lax.fori_loop(0, PR * PC, flip, 0)

    mr = lax.broadcasted_iota(jnp.int32, (256, 256), 0)
    mc = lax.broadcasted_iota(jnp.int32, (256, 256), 1)
    split = jnp.where(
        mr == jnp.where(mc < 128, 2 * mc, 2 * mc - 255), 1.0, 0.0
    ).astype(BF16)

    low = low_rows()

    def unpatch(dst, terms, p, x0):
        blocks = [terms[8 * m : 8 * m + 8] for m in range(K // 8)]
        for c in range(CH):
            for u in range(0, FIELD, 2):
                y = S * p + u
                b0, b1, b2, b3, b4 = blocks[(c * FIELD + u) // 2 * 5 :][:5]
                dst[c, y, pl.ds(x0, 8), :] += b0
                dst[c, y, pl.ds(x0 + 8, 8), :] += b1
                dst[c, y, pl.ds(x0 + 16, 8), :] += jnp.where(low, b2, 0.0)
                dst[c, y + 1, pl.ds(x0 - 4, 8), :] += jnp.where(low, 0.0, b2)
                dst[c, y + 1, pl.ds(x0 + 4, 8), :] += b3
                dst[c, y + 1, pl.ds(x0 + 12, 8), :] += b4

    for c in range(CH):
        pltpu.make_async_copy(rb.at[c], rb.at[c], a2a_recv.at[c]).wait()
        for i in range(4):
            pair = rb.at[c, i].reshape(256, 128)[...]
            turned = lax.dot_general(
                pair, split, (((0,), (0,)), ((), ())), preferred_element_type=F32
            )
            for par in range(2):
                y0 = 8 * i + 4 * par
                part = turned[:, par * 128 : par * 128 + 128].reshape(4, 32, 128)
                ext[c, y0 : y0 + 4, 8:40, :] = part
        lo = 384 * c
        hi = 384 * (c + 1) if c < CH - 1 else K

        def encode(p, carry, c=c, lo=lo, hi=hi):
            zero = lax.shift_right_logical(p, 4)
            for q in range(PC):
                pos = PC * p + q
                columns = patch(ext, p, zero + (8 + S * q), [c])
                pat[pos, 400 * c : 400 * c + 400, :] = columns
                if lo < 400 * c:
                    columns = jnp.concatenate([pat[pos, lo : 400 * c, :], columns], axis=0)
                sums = jnp.dot(wv[pos, :, lo:hi], columns[: hi - lo], preferred_element_type=F32)
                if c > 0:
                    sums = sums + hs[pos]
                if c < CH - 1:
                    hs[pos] = sums
                else:
                    hidden = sums.astype(BF16)
                    hext[p, q + 1] = hidden
                    hid_out[pos] = hidden
            return carry

        lax.fori_loop(0, PR, encode, 0)

    class Exchange:
        def __init__(self, n, axis, src, dst):
            self.axis, self.src, self.dst = axis, src, dst
            self.send, self.recv = sems[2 * n], sems[2 * n + 1]

        def copy(self, side):
            step = 1 if side else -1
            to = (row + step, col) if self.axis == "row" else (row, col + step)
            return pltpu.make_async_remote_copy(
                src_ref=self.src(side),
                dst_ref=self.dst(1 - side),
                send_sem=self.send.at[side],
                recv_sem=self.recv.at[side],
                device_id=to,
                device_id_type=MESH,
            )

        def each(self, act):
            for side in SIDES:

                @pl.when(there(self.axis, side))
                def _(side=side):
                    act(side)

        def start(self):
            self.each(lambda side: self.copy(side).start())

        def arrive(self):
            self.each(lambda side: self.copy(1 - side).wait_recv())

        def sent(self):
            self.each(lambda side: self.copy(side).wait_send())

    def side_columns(ref):
        return (
            lambda side: ref.at[:, 3 if side else 1],
            lambda side: ref.at[:, 4 if side else 0],
        )

    def whole(send, recv):
        return lambda side: send.at[side], lambda side: recv.at[side]

    hidden_x = Exchange(0, "col", *side_columns(hext))
    square_x = Exchange(1, "row", *whole(edge_s, edge_r))
    inverse_x = Exchange(2, "col", *side_columns(iext))
    spread_x = Exchange(3, "row", *whole(spr_s, spr_r))

    half = ROWS // 2

    def crosses(k):
        dr, dc = DIRS[k]
        return row == (half - 1 if dr > 0 else half) if dr and dc else None

    class Around:
        def __init__(self, n, send, recv, through):
            self.bufs, self.sems = (send, recv), sems[n : n + 4]
            self.through = through

        def copy(self, k):
            dr, dc = DIRS[k]
            return pltpu.make_async_remote_copy(
                src_ref=self.bufs[0][k],
                dst_ref=self.bufs[1][7 - k],
                send_sem=self.sems[0].at[k],
                recv_sem=self.sems[1].at[7 - k],
                device_id=(row + dr, col + dc),
                device_id_type=MESH,
            )

        def to_relay(self, k):
            dr, dc = DIRS[k]
            return pltpu.make_async_remote_copy(
                src_ref=self.bufs[0][k],
                dst_ref=self.through[(dc + 1) // 2],
                send_sem=self.sems[0].at[k],
                recv_sem=self.sems[2].at[(dc + 1) // 2],
                device_id=(row - 3 * dr, col),
                device_id_type=MESH,
            )

        def from_relay(self, k):
            dr, dc = DIRS[k]
            return pltpu.make_async_remote_copy(
                src_ref=self.through[(dc + 1) // 2],
                dst_ref=self.bufs[1][7 - k],
                send_sem=self.sems[3].at[(dc + 1) // 2],
                recv_sem=self.sems[1].at[7 - k],
                device_id=(row + half * dr, col + dc),
                device_id_type=MESH,
            )

        def each(self, act):
            for k in range(8):

                @pl.when(near(k))
                def _(k=k):
                    act(k)

        def start(self, which=range(8)):
            for k in which:
                apart = crosses(k)
                if apart is None:

                    @pl.when(near(k))
                    def _(k=k):
                        self.copy(k).start()

                else:

                    @pl.when(near(k) & apart)
                    def _(k=k):
                        self.to_relay(k).start()

                    @pl.when(near(k) & jnp.logical_not(apart))
                    def _(k=k):
                        self.copy(k).start()

        def relays(self, act):
            for k, (dr, dc) in enumerate(DIRS):
                if dr and dc:

                    @pl.when((row == (0 if dr > 0 else ROWS - 1)) & there("col", (dc + 1) // 2))
                    def _(k=k):
                        act(k)

        def relay(self):
            def pass_on(k):
                slot = (DIRS[k][1] + 1) // 2
                held = self.through[slot]
                pltpu.make_async_copy(held, held, self.sems[2].at[slot]).wait()
                self.from_relay(k).start()

            self.relays(pass_on)

        def arrive(self):
            self.each(lambda k: self.copy(7 - k).wait_recv())

        def sent(self):
            self.each(lambda k: self.copy(k).wait_send())
            self.relays(lambda k: self.from_relay(k).wait_send())

    terms_x = Around(8, terms_s, terms_r, terms_t)
    resid_x = Around(12, resid_s, resid_r, resid_t)

    hidden_x.start()

    zero = lax.shift_right_logical(row, 8)

    def pack_rows(src, y0):
        blocks = []
        for c in range(CH):
            for y in range(y0, y0 + 8, 2):
                blocks += [
                    src[c, y, pl.ds(zero + 16, 8), :],
                    jnp.where(low, src[c, y, pl.ds(zero + 24, 8), :], src[c, y + 1, pl.ds(zero + 12, 8), :]),
                    src[c, y + 1, pl.ds(zero + 20, 8), :],
                ]
        return jnp.concatenate(blocks, axis=0).astype(BF16)

    def unpack_rows(got, y0):
        for c in range(CH):
            for n in range(4):
                at = (c * 4 + n) * 24
                yield c, y0 + 2 * n, [got[at + 8 * m : at + 8 * m + 8] for m in range(3)]

    def pack(src, k, ys, xs):
        dr, dc = DIRS[k]
        if dc == 0:
            return pack_rows(src, ys[dr])
        ny = 16 if dr == 0 else 8
        part = src[:, ys[dr] : ys[dr] + ny, pl.ds(zero + xs[dc], 8), :]
        return part.reshape(RIM[k], 128).astype(BF16)

    def send_terms(which):
        for k in which:
            terms_s[k][...] = pack(cext, k, OUTER_Y, OUTER_X)
        terms_x.start(which)

    def decode(p, carry):
        zero = lax.shift_right_logical(p, 4)
        for q in range(PC):
            pos = PC * p + q
            terms = jnp.dot(wt[pos], hid_out[pos], preferred_element_type=F32)
            unpatch(cext, terms, p, zero + (8 + S * q))
        return carry

    lax.fori_loop(0, PR // 2, decode, 0)
    send_terms([k for k in range(8) if DIRS[k][0] < 0])
    lax.fori_loop(PR // 2, PR, decode, 0)
    send_terms([k for k in range(8) if DIRS[k][0] >= 0])

    hidden_x.arrive()

    def across(get):
        cells = [get(b) for b in range(PC + 2)]
        return [cells[b] + cells[b + 1] + cells[b + 2] for b in range(PC)]

    def chunk(n):
        return pl.ds(pl.multiple_of(n * 16, 16), 16)

    def squares(n, carry):
        rows16 = chunk(n)
        for p in range(PR):

            def square(b):
                v = hext[p, b, rows16, :].astype(F32)
                return v * v

            for q, total in enumerate(across(square)):
                flat[p, q, rows16, :] = total
                if p == 0:
                    edge_s[0, q, rows16, :] = total.astype(BF16)
                if p == PR - 1:
                    edge_s[1, q, rows16, :] = total.astype(BF16)
        return carry

    lax.fori_loop(0, F // 16, squares, 0)
    square_x.start()
    terms_x.relay()

    square_x.arrive()

    def down(q, rows16, outside):
        cells = [outside[0, q, rows16, :].astype(F32)]
        cells += [flat[p, q, rows16, :] for p in range(PR)]
        cells += [outside[1, q, rows16, :].astype(F32)]
        return [cells[p] + cells[p + 1] + cells[p + 2] for p in range(PR)]

    def pool(n, carry):
        rows16 = chunk(n)
        for q in range(PC):
            for p, total in enumerate(down(q, rows16, edge_r)):
                energy = jnp.sqrt(1.0 + total)
                iext[p, q + 1, rows16, :] = (1.0 / energy).astype(BF16)
        return carry

    lax.fori_loop(0, F // 16, pool, 0)
    inverse_x.start()

    terms_x.arrive()
    for k, (dr, dc) in enumerate(DIRS):
        got = terms_r[k][...].astype(F32)
        if dc == 0:
            for c, y, (b0, b1, b2) in unpack_rows(got, INNER_Y[dr]):
                cext[c, y, pl.ds(zero + 16, 8), :] += b0
                cext[c, y, pl.ds(zero + 24, 8), :] += jnp.where(low, b1, 0.0)
                cext[c, y + 1, pl.ds(zero + 12, 8), :] += jnp.where(low, 0.0, b1)
                cext[c, y + 1, pl.ds(zero + 20, 8), :] += b2
        else:
            ny = 16 if dr == 0 else 8
            y0 = INNER_Y[dr]
            cext[:, y0 : y0 + ny, pl.ds(zero + INNER_X[dc], 8), :] += got.reshape(CH, ny, 8, 128)
    for x, n in ((16, 8), (24, 4)):
        at = slice(x, x + n)
        resid = cext[:, 8:24, at, :] - ext[:, 8:24, at, :]
        rext[:, 8:24, at, :] = resid.astype(BF16).astype(F32)
    for k in range(8):
        resid_s[k][...] = pack(rext, k, INNER_Y, INNER_X)
    resid_x.start()

    inverse_x.arrive()

    def inverses(n, carry):
        rows16 = chunk(n)
        for p in range(PR):
            for q, total in enumerate(across(lambda b: iext[p, b, rows16, :].astype(F32))):
                flat[p, q, rows16, :] = total
                if p == 0:
                    spr_s[0, q, rows16, :] = total.astype(BF16)
                if p == PR - 1:
                    spr_s[1, q, rows16, :] = total.astype(BF16)
        return carry

    lax.fori_loop(0, F // 16, inverses, 0)
    spread_x.start()
    resid_x.relay()

    resid_x.arrive()
    for k in sorted(range(8), key=lambda k: DIRS[k][1] != 0):
        dr, dc = DIRS[k]
        got = resid_r[k][...].astype(F32)
        if dc == 0:
            for c, y, (b0, b1, b2) in unpack_rows(got, OUTER_Y[dr]):
                rext[c, y, pl.ds(zero + 16, 8), :] = b0
                rext[c, y, pl.ds(zero + 24, 8), :] = b1
                rext[c, y + 1, pl.ds(zero + 12, 8), :] = b1
                rext[c, y + 1, pl.ds(zero + 20, 8), :] = b2
        else:
            ny = 16 if dr == 0 else 8
            y0 = OUTER_Y[dr]
            rext[:, y0 : y0 + ny, pl.ds(zero + OUTER_X[dc], 8), :] = got.reshape(CH, ny, 8, 128)

    def backward(p, carry):
        zero = lax.shift_right_logical(p, 4)
        for q in range(PC):
            pos = PC * p + q
            columns = patch(rext, p, zero + (8 + S * q))
            rpat[pos] = columns
            hs[pos] = jnp.dot(wv[pos], columns, preferred_element_type=F32)
        return carry

    lax.fori_loop(0, PR, backward, 0)

    spread_x.arrive()

    def widen(n, carry):
        rows16 = chunk(n)
        for q in range(PC):
            for p, total in enumerate(down(q, rows16, spr_r)):
                hidden = hid_out[p * PC + q, rows16, :].astype(F32)
                back = SPARSITY * hidden * total + hs[p * PC + q, rows16, :]
                back_out[p * PC + q, rows16, :] = back.astype(BF16)
        return carry

    lax.fori_loop(0, F // 16, widen, 0)

    pltpu.make_async_copy(
        rb.at[:, :, pl.ds(0, DEVS - 1)], rb.at[:, :, pl.ds(0, DEVS - 1)], a2a_send
    ).wait()
    for exchange in (hidden_x, square_x, inverse_x, spread_x, terms_x, resid_x):
        exchange.sent()


def grad_kernel(pat, rpat, back, hid, out, stage, sems):
    halves = (slice(0, K // 2), slice(K // 2, K))
    copies = []
    for pos in range(PR * PC):
        right = jnp.concatenate([back[pos], hid[pos]], axis=1)
        for n, rows in enumerate(halves):
            left = jnp.concatenate([pat[pos, rows, :], rpat[pos, rows, :]], axis=1)
            grad = lax.dot_general(left, right, (((1,), (1,)), ((), ())), preferred_element_type=F32)
            stage[pos, rows, :] = grad * (1.0 / B)
            copy = pltpu.make_async_copy(stage.at[pos, rows], out.at[pos, rows], sems.at[pos, n])
            copy.start()
            copies.append(copy)
    for copy in copies:
        copy.wait()


def main_call(images, weights):
    dma = pltpu.SemaphoreType.DMA
    vmem = pl.BlockSpec(memory_space=pltpu.VMEM)
    hbm = pl.BlockSpec(memory_space=pltpu.HBM)
    n_pos = PR * PC
    return pl.pallas_call(
        main_kernel,
        name="rica_main",
        out_shape=(
            pltpu.VMEM((n_pos, K, B), BF16),
            pltpu.VMEM((n_pos, K, B), BF16),
            pltpu.VMEM((n_pos, F, B), BF16),
            pltpu.VMEM((n_pos, F, B), BF16),
        ),
        in_specs=[hbm, hbm],
        out_specs=(vmem,) * 4,
        scratch_shapes=[
            pltpu.VMEM((n_pos, F, K), BF16),
            pltpu.VMEM((CH, 32, 40, 128), F32),
            pltpu.VMEM((n_pos, F, B), F32),
            pltpu.VMEM((CH, WIDTH, HEIGHT), BF16),
            pltpu.VMEM((n_pos, K, F), BF16),
            pltpu.VMEM((4, WIDTH + 32, 128), F32),
            pltpu.VMEM((COLS, CH, 32, 2, 128), BF16),
            pltpu.VMEM((CH, 4, DEVS, 2, 128), BF16),
            pltpu.VMEM((CH, 32, 40, 128), F32),
            pltpu.VMEM((CH, 32, 40, 128), F32),
            pltpu.VMEM((PR, PC + 2, F, B), BF16),
            pltpu.VMEM((PR, PC + 2, F, B), BF16),
            pltpu.VMEM((PR, PC, F, B), F32),
            *[pltpu.VMEM((2, PC, F, B), BF16) for _ in range(4)],
            *[pltpu.VMEM((n, 128), BF16) for _ in range(4) for n in RIM],
            *[pltpu.VMEM((RIM[0], 128), BF16) for _ in range(4)],
            *[dma for _ in range(3)],
            dma((CH,)),
            *[dma((2,)) for _ in range(8)],
            *[dma((n,)) for _ in range(2) for n in (8, 8, 2, 2)],
        ],
        compiler_params=pltpu.CompilerParams(
            collective_id=0, has_side_effects=True, vmem_limit_bytes=36 * 1024 * 1024
        ),
    )(images, weights)


def grad_call(*factors):
    n_pos = PR * PC
    vmem = pl.BlockSpec(memory_space=pltpu.VMEM)
    return pl.pallas_call(
        grad_kernel,
        name="rica_grad",
        out_shape=jax.ShapeDtypeStruct((n_pos, K, F), F32),
        in_specs=[vmem] * 4,
        out_specs=pl.BlockSpec(memory_space=pltpu.HBM),
        scratch_shapes=[
            pltpu.VMEM((n_pos, K, F), F32),
            pltpu.SemaphoreType.DMA((n_pos, 2)),
        ],
        compiler_params=pltpu.CompilerParams(vmem_limit_bytes=12 * 1024 * 1024),
    )(*factors)


def body(images, weights):
    images = images.reshape(CH, HEIGHT, WIDTH).transpose(0, 2, 1)
    weights = weights.reshape(PR * PC, F, K).transpose(0, 2, 1)
    images = pltpu.with_memory_space_constraint(images, pltpu.HBM)
    weights = pltpu.with_memory_space_constraint(weights, pltpu.HBM)
    factors = main_call(images, weights)
    factors = [pltpu.with_memory_space_constraint(x, pltpu.VMEM) for x in factors]
    grad = grad_call(*factors)
    return grad.transpose(0, 2, 1).reshape(PR, PC, F, K)


def solution(mesh):
    return jax.shard_map(
        body,
        mesh=mesh,
        in_specs=(P(("row", "col"), None, None, None), P("row", "col", None, None)),
        out_specs=P("row", "col", None, None),
        check_vma=False,
    )
```

```python
import jax
import jax.numpy as jnp
from jax import lax
from jax.experimental import pallas as pl
from jax.experimental.pallas import tpu as pltpu
from jax.sharding import PartitionSpec as P

MESH = pl.DeviceIdType.MESH
F32 = jnp.float32
BF16 = jnp.bfloat16

ROWS, COLS = 8, 16
DEVS = ROWS * COLS
CH, S, FIELD, PAD = 3, 4, 20, 8
K = 1200
F = 128
B = 128
HEIGHT, WIDTH = 128, 192
PR, PC = 4, 3
SPARSITY = 0.5
EPS = 1e-05

SIDES = (0, 1)
DIRS = [(dr, dc) for dr in (-1, 0, 1) for dc in (-1, 0, 1) if (dr, dc) != (0, 0)]
OUTER_Y, OUTER_X = {-1: 0, 0: 8, 1: 24}, {-1: 8, 1: 28}
INNER_Y, INNER_X = {-1: 8, 0: 8, 1: 16}, {-1: 16, 1: 20}
RIM = [CH * (288 // CH if dc == 0 else 8 * (16 if dr == 0 else 8)) for dr, dc in DIRS]


def low_rows():
    return lax.broadcasted_iota(jnp.int32, (8, 128), 0) < 4


def patch(src, p, x0, channels=range(CH)):
    low = low_rows()
    blocks = []
    for c in channels:
        for u in range(0, FIELD, 2):
            y = S * p + u
            blocks += [
                src[c, y, pl.ds(x0, 8), :],
                src[c, y, pl.ds(x0 + 8, 8), :],
                jnp.where(low, src[c, y, pl.ds(x0 + 16, 8), :], src[c, y + 1, pl.ds(x0 - 4, 8), :]),
                src[c, y + 1, pl.ds(x0 + 4, 8), :],
                src[c, y + 1, pl.ds(x0 + 12, 8), :],
            ]
    return jnp.concatenate(blocks, axis=0).astype(BF16)


def main_kernel(img_hbm, w_hbm, pat, rpat, back_out, hid_out, *scr):
    (wv, rext, hs, img, wt, strip, sb, rb, ext, cext, hext, iext, flat, edge_s, edge_r, spr_s, spr_r) = scr[:17]
    terms_s, terms_r, resid_s, resid_r = scr[17:25], scr[25:33], scr[33:41], scr[41:49]
    terms_t, resid_t = scr[49:51], scr[51:53]
    im_sem, w_sem, a2a_send, a2a_recv = scr[53:57]
    sems = scr[57:]
    row = lax.axis_index("row")
    col = lax.axis_index("col")
    me = row * COLS + col

    im_copy = pltpu.make_async_copy(img_hbm, img, im_sem)
    im_copy.start()

    def there(axis, side):
        at, n = (row, ROWS) if axis == "row" else (col, COLS)
        return at < n - 1 if side else at > 0

    barrier = pltpu.get_barrier_semaphore()

    def greet(i, carry):
        tr = (row + i) & (ROWS - 1)
        for j in range(COLS):
            pl.semaphore_signal(
                barrier, inc=1, device_id=(tr, (col + j) & (COLS - 1)), device_id_type=MESH
            )
        return carry

    lax.fori_loop(2, ROWS, greet, 0)
    greet(1, 0)
    for j in range(1, COLS):
        pl.semaphore_signal(
            barrier, inc=1, device_id=(row, (col + j) & (COLS - 1)), device_id_type=MESH
        )

    w_copy = pltpu.make_async_copy(w_hbm, wt, w_sem)
    w_copy.start()

    im_copy.wait()
    pixels = img[...].reshape(CH * WIDTH, HEIGHT).astype(F32)
    count = CH * HEIGHT * WIDTH
    center = jnp.sum(pixels, axis=(0, 1), keepdims=True) / count
    shifted = pixels - center
    variance = jnp.sum(shifted * shifted, axis=(0, 1), keepdims=True) / count
    normed = (shifted / jnp.sqrt(variance + EPS)).astype(BF16)

    planes = jnp.concatenate([normed[c * WIDTH : (c + 1) * WIDTH] for c in range(CH)], axis=1)
    yy = lax.broadcasted_iota(jnp.int32, (HEIGHT, 128), 0)
    lane = lax.broadcasted_iota(jnp.int32, (HEIGHT, 128), 1)
    where_from = []
    for c in range(CH):
        offset = jnp.where((lane >> 5) == c, yy - 4 * (lane & 31), -1)
        where_from.append(
            jnp.concatenate([jnp.where(offset == j, 1.0, 0.0) for j in range(4)], axis=1)
        )
    spread_y = jnp.concatenate(where_from, axis=0).astype(BF16)
    strips = jnp.dot(planes, spread_y, preferred_element_type=F32)
    for j in range(4):
        strip[j, 0:8, :] = jnp.zeros((8, 128), F32)
        strip[j, 8 : 8 + WIDTH, :] = strips[:, j * 128 : j * 128 + 128]
        strip[j, 8 + WIDTH : 32 + WIDTH, :] = jnp.zeros((24, 128), F32)

    def cut(t, carry):
        parts = [strip[j, pl.ds(12 * t, 32), :] for j in range(4)]
        block = jnp.concatenate(parts, axis=0).astype(BF16).T
        view = sb.at[t].reshape(CH * 64, 128)
        for c in range(CH):
            view[c * 64 : c * 64 + 16, :] = jnp.zeros((16, 128), BF16)
            view[c * 64 + 16 : c * 64 + 48, :] = block[c * 32 : c * 32 + 32]
            view[c * 64 + 48 : c * 64 + 64, :] = jnp.zeros((16, 128), BF16)
        return carry

    lax.fori_loop(0, COLS, cut, 0)

    pl.semaphore_wait(barrier, DEVS - 1)

    def send_block(c, tr, tc):
        pltpu.make_async_remote_copy(
            src_ref=sb.at[tc, c, pl.ds(7 + 2 * tr, 4)],
            dst_ref=rb.at[c, :, me],
            send_sem=a2a_send,
            recv_sem=a2a_recv.at[c],
            device_id=(tr, tc),
            device_id_type=MESH,
        ).start()

    for c in range(CH):
        pltpu.make_async_copy(
            sb.at[col, c, pl.ds(7 + 2 * row, 4)], rb.at[c, :, me], a2a_recv.at[c]
        ).start()

        def send_row(i, carry, c=c):
            tr = (row + i) & (ROWS - 1)
            for j in range(COLS):
                send_block(c, tr, (col + j) & (COLS - 1))
            return carry

        lax.fori_loop(1, ROWS, send_row, 0)
        for j in range(1, COLS):
            send_block(c, row, (col + j) & (COLS - 1))

    for side in SIDES:

        @pl.when(jnp.logical_not(there("col", side)))
        def _(side=side):
            for p in range(PR):
                hext[p, 4 * side] = jnp.zeros((F, B), BF16)
                iext[p, 4 * side] = jnp.zeros((F, B), BF16)

        @pl.when(jnp.logical_not(there("row", side)))
        def _(side=side):
            for ref in (edge_r, spr_r):
                ref[side] = jnp.zeros(ref.shape[1:], BF16)

    def near(k):
        dr, dc = DIRS[k]
        ok = None
        for axis, d in (("row", dr), ("col", dc)):
            if d:
                one = there(axis, (d + 1) // 2)
                ok = one if ok is None else ok & one
        return ok

    for k in range(8):

        @pl.when(jnp.logical_not(near(k)))
        def _(k=k):
            for ref in (terms_r[k], resid_r[k]):
                ref[...] = jnp.zeros(ref.shape, BF16)

    cext[...] = jnp.zeros(cext.shape, F32)
    w_copy.wait()

    def flip(pos, carry):
        for kb in range(0, K, 128):
            n = min(128, K - kb)
            wv[pos, :, kb : kb + n] = wt[pos, kb : kb + n, :].T
        return carry

    lax.fori_loop(0, PR * PC, flip, 0)

    mr = lax.broadcasted_iota(jnp.int32, (256, 256), 0)
    mc = lax.broadcasted_iota(jnp.int32, (256, 256), 1)
    split = jnp.where(
        mr == jnp.where(mc < 128, 2 * mc, 2 * mc - 255), 1.0, 0.0
    ).astype(BF16)

    low = low_rows()

    def unpatch(dst, terms, p, x0):
        blocks = [terms[8 * m : 8 * m + 8] for m in range(K // 8)]
        for c in range(CH):
            for u in range(0, FIELD, 2):
                y = S * p + u
                b0, b1, b2, b3, b4 = blocks[(c * FIELD + u) // 2 * 5 :][:5]
                dst[c, y, pl.ds(x0, 8), :] += b0
                dst[c, y, pl.ds(x0 + 8, 8), :] += b1
                dst[c, y, pl.ds(x0 + 16, 8), :] += jnp.where(low, b2, 0.0)
                dst[c, y + 1, pl.ds(x0 - 4, 8), :] += jnp.where(low, 0.0, b2)
                dst[c, y + 1, pl.ds(x0 + 4, 8), :] += b3
                dst[c, y + 1, pl.ds(x0 + 12, 8), :] += b4

    for c in range(CH):
        pltpu.make_async_copy(rb.at[c], rb.at[c], a2a_recv.at[c]).wait()
        for i in range(4):
            pair = rb.at[c, i].reshape(256, 128)[...]
            turned = lax.dot_general(
                pair, split, (((0,), (0,)), ((), ())), preferred_element_type=F32
            )
            for par in range(2):
                y0 = 8 * i + 4 * par
                part = turned[:, par * 128 : par * 128 + 128].reshape(4, 32, 128)
                ext[c, y0 : y0 + 4, 8:40, :] = part
        lo = 384 * c
        hi = 384 * (c + 1) if c < CH - 1 else K

        def encode(p, carry, c=c, lo=lo, hi=hi):
            zero = lax.shift_right_logical(p, 4)
            for q in range(PC):
                pos = PC * p + q
                columns = patch(ext, p, zero + (8 + S * q), [c])
                pat[pos, 400 * c : 400 * c + 400, :] = columns
                if lo < 400 * c:
                    columns = jnp.concatenate([pat[pos, lo : 400 * c, :], columns], axis=0)
                sums = jnp.dot(wv[pos, :, lo:hi], columns[: hi - lo], preferred_element_type=F32)
                if c > 0:
                    sums = sums + hs[pos]
                if c < CH - 1:
                    hs[pos] = sums
                else:
                    hidden = sums.astype(BF16)
                    hext[p, q + 1] = hidden
                    hid_out[pos] = hidden
            return carry

        lax.fori_loop(0, PR, encode, 0)

    class Exchange:
        def __init__(self, n, axis, src, dst):
            self.axis, self.src, self.dst = axis, src, dst
            self.send, self.recv = sems[2 * n], sems[2 * n + 1]

        def copy(self, side):
            step = 1 if side else -1
            to = (row + step, col) if self.axis == "row" else (row, col + step)
            return pltpu.make_async_remote_copy(
                src_ref=self.src(side),
                dst_ref=self.dst(1 - side),
                send_sem=self.send.at[side],
                recv_sem=self.recv.at[side],
                device_id=to,
                device_id_type=MESH,
            )

        def each(self, act):
            for side in SIDES:

                @pl.when(there(self.axis, side))
                def _(side=side):
                    act(side)

        def start(self):
            self.each(lambda side: self.copy(side).start())

        def arrive(self):
            self.each(lambda side: self.copy(1 - side).wait_recv())

        def sent(self):
            self.each(lambda side: self.copy(side).wait_send())

    def side_columns(ref):
        return (
            lambda side: ref.at[:, 3 if side else 1],
            lambda side: ref.at[:, 4 if side else 0],
        )

    def whole(send, recv):
        return lambda side: send.at[side], lambda side: recv.at[side]

    hidden_x = Exchange(0, "col", *side_columns(hext))
    square_x = Exchange(1, "row", *whole(edge_s, edge_r))
    inverse_x = Exchange(2, "col", *side_columns(iext))
    spread_x = Exchange(3, "row", *whole(spr_s, spr_r))

    half = ROWS // 2

    def crosses(k):
        dr, dc = DIRS[k]
        return row == (half - 1 if dr > 0 else half) if dr and dc else None

    class Around:
        def __init__(self, n, send, recv, through):
            self.bufs, self.sems = (send, recv), sems[n : n + 4]
            self.through = through

        def copy(self, k):
            dr, dc = DIRS[k]
            return pltpu.make_async_remote_copy(
                src_ref=self.bufs[0][k],
                dst_ref=self.bufs[1][7 - k],
                send_sem=self.sems[0].at[k],
                recv_sem=self.sems[1].at[7 - k],
                device_id=(row + dr, col + dc),
                device_id_type=MESH,
            )

        def to_relay(self, k):
            dr, dc = DIRS[k]
            return pltpu.make_async_remote_copy(
                src_ref=self.bufs[0][k],
                dst_ref=self.through[(dc + 1) // 2],
                send_sem=self.sems[0].at[k],
                recv_sem=self.sems[2].at[(dc + 1) // 2],
                device_id=(row - 3 * dr, col),
                device_id_type=MESH,
            )

        def from_relay(self, k):
            dr, dc = DIRS[k]
            return pltpu.make_async_remote_copy(
                src_ref=self.through[(dc + 1) // 2],
                dst_ref=self.bufs[1][7 - k],
                send_sem=self.sems[3].at[(dc + 1) // 2],
                recv_sem=self.sems[1].at[7 - k],
                device_id=(row + half * dr, col + dc),
                device_id_type=MESH,
            )

        def each(self, act):
            for k in range(8):

                @pl.when(near(k))
                def _(k=k):
                    act(k)

        def start(self, which=range(8)):
            for k in which:
                apart = crosses(k)
                if apart is None:

                    @pl.when(near(k))
                    def _(k=k):
                        self.copy(k).start()

                else:

                    @pl.when(near(k) & apart)
                    def _(k=k):
                        self.to_relay(k).start()

                    @pl.when(near(k) & jnp.logical_not(apart))
                    def _(k=k):
                        self.copy(k).start()

        def relays(self, act):
            for k, (dr, dc) in enumerate(DIRS):
                if dr and dc:

                    @pl.when((row == (0 if dr > 0 else ROWS - 1)) & there("col", (dc + 1) // 2))
                    def _(k=k):
                        act(k)

        def relay(self):
            def pass_on(k):
                slot = (DIRS[k][1] + 1) // 2
                held = self.through[slot]
                pltpu.make_async_copy(held, held, self.sems[2].at[slot]).wait()
                self.from_relay(k).start()

            self.relays(pass_on)

        def arrive(self):
            self.each(lambda k: self.copy(7 - k).wait_recv())

        def sent(self):
            self.each(lambda k: self.copy(k).wait_send())
            self.relays(lambda k: self.from_relay(k).wait_send())

    terms_x = Around(8, terms_s, terms_r, terms_t)
    resid_x = Around(12, resid_s, resid_r, resid_t)

    hidden_x.start()

    zero = lax.shift_right_logical(row, 8)

    def pack_rows(src, y0):
        blocks = []
        for c in range(CH):
            for y in range(y0, y0 + 8, 2):
                blocks += [
                    src[c, y, pl.ds(zero + 16, 8), :],
                    jnp.where(low, src[c, y, pl.ds(zero + 24, 8), :], src[c, y + 1, pl.ds(zero + 12, 8), :]),
                    src[c, y + 1, pl.ds(zero + 20, 8), :],
                ]
        return jnp.concatenate(blocks, axis=0).astype(BF16)

    def unpack_rows(got, y0):
        for c in range(CH):
            for n in range(4):
                at = (c * 4 + n) * 24
                yield c, y0 + 2 * n, [got[at + 8 * m : at + 8 * m + 8] for m in range(3)]

    def pack(src, k, ys, xs):
        dr, dc = DIRS[k]
        if dc == 0:
            return pack_rows(src, ys[dr])
        ny = 16 if dr == 0 else 8
        part = src[:, ys[dr] : ys[dr] + ny, pl.ds(zero + xs[dc], 8), :]
        return part.reshape(RIM[k], 128).astype(BF16)

    def send_terms(which):
        for k in which:
            terms_s[k][...] = pack(cext, k, OUTER_Y, OUTER_X)
        terms_x.start(which)

    def decode(p, carry):
        zero = lax.shift_right_logical(p, 4)
        for q in range(PC):
            pos = PC * p + q
            terms = jnp.dot(wt[pos], hid_out[pos], preferred_element_type=F32)
            unpatch(cext, terms, p, zero + (8 + S * q))
        return carry

    lax.fori_loop(0, PR // 2, decode, 0)
    send_terms([k for k in range(8) if DIRS[k][0] < 0])
    lax.fori_loop(PR // 2, PR, decode, 0)
    send_terms([k for k in range(8) if DIRS[k][0] >= 0])

    hidden_x.arrive()

    def across(get):
        cells = [get(b) for b in range(PC + 2)]
        return [cells[b] + cells[b + 1] + cells[b + 2] for b in range(PC)]

    def chunk(n):
        return pl.ds(pl.multiple_of(n * 16, 16), 16)

    def squares(n, carry):
        rows16 = chunk(n)
        for p in range(PR):

            def square(b):
                v = hext[p, b, rows16, :].astype(F32)
                return v * v

            for q, total in enumerate(across(square)):
                flat[p, q, rows16, :] = total
                if p == 0:
                    edge_s[0, q, rows16, :] = total.astype(BF16)
                if p == PR - 1:
                    edge_s[1, q, rows16, :] = total.astype(BF16)
        return carry

    lax.fori_loop(0, F // 16, squares, 0)
    square_x.start()
    terms_x.relay()

    square_x.arrive()

    def down(q, rows16, outside):
        cells = [outside[0, q, rows16, :].astype(F32)]
        cells += [flat[p, q, rows16, :] for p in range(PR)]
        cells += [outside[1, q, rows16, :].astype(F32)]
        return [cells[p] + cells[p + 1] + cells[p + 2] for p in range(PR)]

    def pool(n, carry):
        rows16 = chunk(n)
        for q in range(PC):
            for p, total in enumerate(down(q, rows16, edge_r)):
                energy = jnp.sqrt(1.0 + total)
                iext[p, q + 1, rows16, :] = (1.0 / energy).astype(BF16)
        return carry

    lax.fori_loop(0, F // 16, pool, 0)
    inverse_x.start()

    terms_x.arrive()
    for k, (dr, dc) in enumerate(DIRS):
        got = terms_r[k][...].astype(F32)
        if dc == 0:
            for c, y, (b0, b1, b2) in unpack_rows(got, INNER_Y[dr]):
                cext[c, y, pl.ds(zero + 16, 8), :] += b0
                cext[c, y, pl.ds(zero + 24, 8), :] += jnp.where(low, b1, 0.0)
                cext[c, y + 1, pl.ds(zero + 12, 8), :] += jnp.where(low, 0.0, b1)
                cext[c, y + 1, pl.ds(zero + 20, 8), :] += b2
        else:
            ny = 16 if dr == 0 else 8
            y0 = INNER_Y[dr]
            cext[:, y0 : y0 + ny, pl.ds(zero + INNER_X[dc], 8), :] += got.reshape(CH, ny, 8, 128)
    for x, n in ((16, 8), (24, 4)):
        at = slice(x, x + n)
        resid = cext[:, 8:24, at, :] - ext[:, 8:24, at, :]
        rext[:, 8:24, at, :] = resid.astype(BF16).astype(F32)
    for k in range(8):
        resid_s[k][...] = pack(rext, k, INNER_Y, INNER_X)
    resid_x.start()

    inverse_x.arrive()

    def inverses(n, carry):
        rows16 = chunk(n)
        for p in range(PR):
            for q, total in enumerate(across(lambda b: iext[p, b, rows16, :].astype(F32))):
                flat[p, q, rows16, :] = total
                if p == 0:
                    spr_s[0, q, rows16, :] = total.astype(BF16)
                if p == PR - 1:
                    spr_s[1, q, rows16, :] = total.astype(BF16)
        return carry

    lax.fori_loop(0, F // 16, inverses, 0)
    spread_x.start()
    resid_x.relay()

    resid_x.arrive()
    for k in sorted(range(8), key=lambda k: DIRS[k][1] != 0):
        dr, dc = DIRS[k]
        got = resid_r[k][...].astype(F32)
        if dc == 0:
            for c, y, (b0, b1, b2) in unpack_rows(got, OUTER_Y[dr]):
                rext[c, y, pl.ds(zero + 16, 8), :] = b0
                rext[c, y, pl.ds(zero + 24, 8), :] = b1
                rext[c, y + 1, pl.ds(zero + 12, 8), :] = b1
                rext[c, y + 1, pl.ds(zero + 20, 8), :] = b2
        else:
            ny = 16 if dr == 0 else 8
            y0 = OUTER_Y[dr]
            rext[:, y0 : y0 + ny, pl.ds(zero + OUTER_X[dc], 8), :] = got.reshape(CH, ny, 8, 128)

    def backward(p, carry):
        zero = lax.shift_right_logical(p, 4)
        for q in range(PC):
            pos = PC * p + q
            columns = patch(rext, p, zero + (8 + S * q))
            rpat[pos] = columns
            hs[pos] = jnp.dot(wv[pos], columns, preferred_element_type=F32)
        return carry

    lax.fori_loop(0, PR, backward, 0)

    spread_x.arrive()

    def widen(n, carry):
        rows16 = chunk(n)
        for q in range(PC):
            for p, total in enumerate(down(q, rows16, spr_r)):
                hidden = hid_out[p * PC + q, rows16, :].astype(F32)
                back = SPARSITY * hidden * total + hs[p * PC + q, rows16, :]
                back_out[p * PC + q, rows16, :] = back.astype(BF16)
        return carry

    lax.fori_loop(0, F // 16, widen, 0)

    pltpu.make_async_copy(
        rb.at[:, :, pl.ds(0, DEVS - 1)], rb.at[:, :, pl.ds(0, DEVS - 1)], a2a_send
    ).wait()
    for exchange in (hidden_x, square_x, inverse_x, spread_x, terms_x, resid_x):
        exchange.sent()


def grad_kernel(pat, rpat, back, hid, out, stage, sems):
    halves = (slice(0, K // 2), slice(K // 2, K))
    copies = []
    for pos in range(PR * PC):
        right = jnp.concatenate([back[pos], hid[pos]], axis=1)
        for n, rows in enumerate(halves):
            left = jnp.concatenate([pat[pos, rows, :], rpat[pos, rows, :]], axis=1)
            grad = lax.dot_general(left, right, (((1,), (1,)), ((), ())), preferred_element_type=F32)
            stage[pos, rows, :] = grad * (1.0 / B)
            copy = pltpu.make_async_copy(stage.at[pos, rows], out.at[pos, rows], sems.at[pos, n])
            copy.start()
            copies.append(copy)
    for copy in copies:
        copy.wait()


def main_call(images, weights):
    dma = pltpu.SemaphoreType.DMA
    vmem = pl.BlockSpec(memory_space=pltpu.VMEM)
    hbm = pl.BlockSpec(memory_space=pltpu.HBM)
    n_pos = PR * PC
    return pl.pallas_call(
        main_kernel,
        name="rica_main",
        out_shape=(
            pltpu.VMEM((n_pos, K, B), BF16),
            pltpu.VMEM((n_pos, K, B), BF16),
            pltpu.VMEM((n_pos, F, B), BF16),
            pltpu.VMEM((n_pos, F, B), BF16),
        ),
        in_specs=[hbm, hbm],
        out_specs=(vmem,) * 4,
        scratch_shapes=[
            pltpu.VMEM((n_pos, F, K), BF16),
            pltpu.VMEM((CH, 32, 40, 128), F32),
            pltpu.VMEM((n_pos, F, B), F32),
            pltpu.VMEM((CH, WIDTH, HEIGHT), BF16),
            pltpu.VMEM((n_pos, K, F), BF16),
            pltpu.VMEM((4, WIDTH + 32, 128), F32),
            pltpu.VMEM((COLS, CH, 32, 2, 128), BF16),
            pltpu.VMEM((CH, 4, DEVS, 2, 128), BF16),
            pltpu.VMEM((CH, 32, 40, 128), F32),
            pltpu.VMEM((CH, 32, 40, 128), F32),
            pltpu.VMEM((PR, PC + 2, F, B), BF16),
            pltpu.VMEM((PR, PC + 2, F, B), BF16),
            pltpu.VMEM((PR, PC, F, B), F32),
            *[pltpu.VMEM((2, PC, F, B), BF16) for _ in range(4)],
            *[pltpu.VMEM((n, 128), BF16) for _ in range(4) for n in RIM],
            *[pltpu.VMEM((RIM[0], 128), BF16) for _ in range(4)],
            *[dma for _ in range(3)],
            dma((CH,)),
            *[dma((2,)) for _ in range(8)],
            *[dma((n,)) for _ in range(2) for n in (8, 8, 2, 2)],
        ],
        compiler_params=pltpu.CompilerParams(
            collective_id=0, has_side_effects=True, vmem_limit_bytes=36 * 1024 * 1024
        ),
    )(images, weights)


def grad_call(*factors):
    n_pos = PR * PC
    vmem = pl.BlockSpec(memory_space=pltpu.VMEM)
    return pl.pallas_call(
        grad_kernel,
        name="rica_grad",
        out_shape=jax.ShapeDtypeStruct((n_pos, K, F), F32),
        in_specs=[vmem] * 4,
        out_specs=pl.BlockSpec(memory_space=pltpu.HBM),
        scratch_shapes=[
            pltpu.VMEM((n_pos, K, F), F32),
            pltpu.SemaphoreType.DMA((n_pos, 2)),
        ],
        compiler_params=pltpu.CompilerParams(vmem_limit_bytes=12 * 1024 * 1024),
    )(*factors)


def body(images, weights):
    images = images.reshape(CH, HEIGHT, WIDTH).transpose(0, 2, 1)
    weights = weights.reshape(PR * PC, F, K).transpose(0, 2, 1)
    images = pltpu.with_memory_space_constraint(images, pltpu.HBM)
    weights = pltpu.with_memory_space_constraint(weights, pltpu.HBM)
    factors = main_call(images, weights)
    factors = [pltpu.with_memory_space_constraint(x, pltpu.VMEM) for x in factors]
    grad = grad_call(*factors)
    return grad.transpose(0, 2, 1).reshape(PR, PC, F, K)


def solution(mesh):
    return jax.shard_map(
        body,
        mesh=mesh,
        in_specs=(P(("row", "col"), None, None, None), P("row", "col", None, None)),
        out_specs=P("row", "col", None, None),
        check_vma=False,
    )
```
